512 devices in a mesh: scen: 64 (over y, x, core), col: 8 (over z).
Axes of the slice: x: 4, y: 8, z: 8, core: 2. Of those that a mesh axis runs over, the one named last changes fastest.
Arguments:
- adaptive_matrices: bfloat16 [128, 512, 8192], P('scen', None, 'col'), may hold values from -0.0625 to 0.0625
- barrier_ratios: bfloat16 [128, 8192], P('scen', 'col'), may hold values from 0.099609375 to 10
- damping_shift: bfloat16 [128, 512], P('scen'), may hold values from 0.5 to 2
- coupler_matrices: bfloat16 [128, 512, 512], P('scen'), may hold values from -0.25 to 0.25
- constraint_bounds: bfloat16 [128, 512], P('scen'), may hold values from -12 to 12
- leading_main_entries: float32 [512], replicated, may hold values from 1 to 8
- leading_source_vector: float32 [512], replicated, may hold values from -24 to 24
- outcome_tallies: int32 [64], replicated, may hold values from 0 to 2, as said below
Outputs:
- first_dir: float32 [512], replicated
- multiplier_update: float32 [128, 512], P('scen')
- adaptive_update: float32 [128, 8192], P('scen', 'col')
The draws below stay inside these ranges and needn't reach their ends.
Inputs may be any that keep to these rules, and one draw needn't show every extreme that they name: `outcome_tallies`: in each aligned block of four consecutive groups the counts sum to 2, a group holding 2 is followed by a group holding 0 inside the same block, and some group holds 2.
All inputs are finite; a program needn't handle non-finite values.
Results may differ from the reference program's by a relative error of at most 0.0034.
Values may be sent and summed in bfloat16 or wider, within the bound.
No kernel may reach another device: no remote copies, remote signals or barrier semaphores. Data moves between devices by JAX's collectives and lax.ppermute only.
A program may use at most 64 MiB of HBM per device.

```python
import math
import jax
import jax.numpy as jnp
import numpy as np
from jax import lax

M = 512
SECOND_VARIABLES = 8192
N0 = 512
BATCH_CAPACITY = 2
BATCH_TOTAL = 64


def draw_outcome_tallies(key, part):
    patterns = jnp.array(np.array([[2, 0, 0, 0], [0, 2, 0, 0], [0, 0, 2, 0], [1, 1, 0, 0], [1, 0, 1, 0], [1, 0, 0, 1], [0, 1, 1, 0], [0, 1, 0, 1], [0, 0, 1, 1]], dtype=np.int32))
    blocks = BATCH_TOTAL // 4
    chosen = jax.random.randint(jax.random.fold_in(key, 11), (blocks,), 0, 9)
    leading = jax.random.randint(jax.random.fold_in(key, 12), (1,), 0, 3)
    chosen = chosen.at[0].set(leading[0])
    return patterns[chosen].reshape(-1).astype(jnp.int32)


def block_scale(stream_key, extent, cuts, smallest, top_value):
    loudness, own = 1.0, jax.random.fold_in(stream_key, 6)
    for axis_at, shards_of in cuts:
        draws = jnp.exp(jax.random.uniform(jax.random.fold_in(own, axis_at), (shards_of,), jnp.float32, smallest / len(cuts), top_value / len(cuts)))
        loudness = loudness * jnp.repeat(draws, extent[axis_at] // shards_of).reshape([-1 if axis == axis_at else 1 for axis in range(len(extent))])
    return loudness


def normal_values(own_key, dims, scale, reach, shards=(), kind=jnp.bfloat16):
    values = scale * jax.random.normal(own_key, dims, jnp.float32)
    if shards:
        values = values * block_scale(own_key, dims, shards, -0.22, 0.18)
    return jnp.clip(values, -reach, reach).astype(kind)


def setup_inputs(seed: int = 0) -> dict:
    key_list = jax.random.split(jax.random.key(seed), 9)
    adaptive_matrices = normal_values(key_list[0], (BATCH_TOTAL * BATCH_CAPACITY, M, SECOND_VARIABLES), SECOND_VARIABLES ** -0.5, 0.0625, ((0, 64), (2, 8)))
    barrier_ratios = jnp.clip(jnp.exp(math.log(10.0) - 4.609084 * jax.random.uniform(key_list[1], (BATCH_TOTAL * BATCH_CAPACITY, SECOND_VARIABLES), jnp.float32) ** block_scale(key_list[1], (BATCH_TOTAL * BATCH_CAPACITY, SECOND_VARIABLES), ((0, 64), (1, 8)), -0.2, 0.2)), 0.099609375, 10.0).astype(jnp.bfloat16)
    damping_shift = jnp.clip(jnp.exp(math.log(2.0) - 1.3862944 * jax.random.uniform(key_list[2], (BATCH_TOTAL * BATCH_CAPACITY, M), jnp.float32) ** block_scale(key_list[2], (BATCH_TOTAL * BATCH_CAPACITY, M), ((0, 64),), -0.2, 0.2)), 0.5, 2.0).astype(jnp.bfloat16)
    coupler_matrices = normal_values(key_list[3], (BATCH_TOTAL * BATCH_CAPACITY, M, N0), M ** -0.5, 0.25, ((0, 64),))
    constraint_bounds = normal_values(key_list[4], (BATCH_TOTAL * BATCH_CAPACITY, M), 2.0, 12.0, ((0, 64),))
    leading_main_entries = jnp.clip(jnp.exp(jax.random.uniform(key_list[5], (N0,), jnp.float32, math.log(1.0), math.log(8.0))), 1.0, 8.0)
    leading_source_vector = normal_values(key_list[6], (N0,), 4.0, 24.0, (), jnp.float32)
    outcome_tallies = draw_outcome_tallies(jax.random.fold_in(key_list[8], 71), 0)
    return {"adaptive_matrices": adaptive_matrices, "barrier_ratios": barrier_ratios, "damping_shift": damping_shift, "coupler_matrices": coupler_matrices, "constraint_bounds": constraint_bounds, "leading_main_entries": leading_main_entries, "leading_source_vector": leading_source_vector, "outcome_tallies": outcome_tallies}


HIGHEST = lax.Precision.HIGHEST

def tri_solve(factor_low, values, transpose_it):
    return lax.linalg.triangular_solve(factor_low, values, left_side=True, lower=True, transpose_a=transpose_it)

def spd_solve(factor_low, values):
    return tri_solve(factor_low, tri_solve(factor_low, values, False), True)

def gram_part(matrix, scaling):
    scaled = (matrix.astype(jnp.float32) * scaling.astype(jnp.float32)[None, :]).astype(jnp.bfloat16)
    return lax.dot_general(scaled.astype(jnp.float32), matrix.astype(jnp.float32), (((1,), (1,)), ((), ())), preferred_element_type=jnp.float32)

def cholesky_of(gram, regular):
    return jnp.linalg.cholesky(gram + jnp.diag(regular.astype(jnp.float32)))

def transposed_dot(left_side, right_side):
    return lax.dot_general(left_side.astype(jnp.float32), right_side.astype(jnp.float32), (((0,), (0,)), ((), ())), precision=HIGHEST, preferred_element_type=jnp.float32)

def reference(adaptive_matrices, barrier_ratios, damping_shift, coupler_matrices, constraint_bounds, leading_main_entries, leading_source_vector, outcome_tallies):
    slot_total = BATCH_TOTAL * BATCH_CAPACITY
    indices = jnp.arange(slot_total, dtype=jnp.int32)
    occupied_markers = indices % BATCH_CAPACITY < outcome_tallies[indices // BATCH_CAPACITY]

    def lower_substitution(running, slice_data):
        matrix, scaling, regular, coupling, target, is_live = slice_data

        def live_case(operand):
            factor_low = cholesky_of(gram_part(matrix, scaling), regular)
            dense_link = coupling.astype(jnp.float32)
            solved = tri_solve(factor_low, dense_link, False)
            second = spd_solve(factor_low, target.astype(jnp.float32)[:, None])
            return (factor_low, transposed_dot(solved, solved), transposed_dot(dense_link, second)[:, 0])

        def spare_case(operand):
            return (jnp.zeros((M, M), jnp.float32), jnp.zeros((N0, N0), jnp.float32), jnp.zeros((N0,), jnp.float32))
        factor_low, schur_term, rhs_term = lax.cond(is_live, live_case, spare_case, 0)
        return ((running[0] + schur_term, running[1] + rhs_term), factor_low)
    starting_state = (jnp.zeros((N0, N0), jnp.float32), jnp.zeros((N0,), jnp.float32))
    (reduced_matrix_total, source_vector_total), triangle_matrices = lax.scan(lower_substitution, starting_state, (adaptive_matrices, barrier_ratios, damping_shift, coupler_matrices, constraint_bounds, occupied_markers))
    schur_full = reduced_matrix_total + jnp.diag(leading_main_entries)
    first_dir = spd_solve(jnp.linalg.cholesky(schur_full), (leading_source_vector - source_vector_total)[:, None])[:, 0]

    def upper_substitution(running, slice_data):
        matrix, scaling, coupling, target, factor_low, is_live = slice_data

        def live_case(operand):
            pushed = target.astype(jnp.float32) + jnp.dot(coupling.astype(jnp.float32), first_dir, precision=HIGHEST)
            dual_vec = spd_solve(factor_low, pushed[:, None])[:, 0]
            primal = scaling.astype(jnp.float32) * jnp.dot(dual_vec.astype(jnp.bfloat16).astype(jnp.float32), matrix.astype(jnp.float32), preferred_element_type=jnp.float32)
            return (dual_vec, primal)

        def spare_case(operand):
            return (jnp.zeros((M,), jnp.float32), jnp.zeros((SECOND_VARIABLES,), jnp.float32))
        return (running, lax.cond(is_live, live_case, spare_case, 0))
    discarded_state, (multiplier_update, adaptive_update) = lax.scan(upper_substitution, jnp.zeros((), jnp.float32), (adaptive_matrices, barrier_ratios, coupler_matrices, constraint_bounds, triangle_matrices, occupied_markers))
    return (first_dir, multiplier_update, adaptive_update)
```

```python
import functools

import jax
import jax.numpy as jnp
from jax import lax
from jax.experimental import pallas as pl
from jax.experimental.pallas import tpu as pltpu
from jax.sharding import PartitionSpec as P

F32 = jnp.float32
BF16 = jnp.bfloat16
B = 128
TOL2 = 1e-12
MAX_STEPS = 4096


def blocks_of(rows):
    n = rows // B
    return [(i, j) for i in range(n) for j in range(i + 1)]


def mm(a, b):
    return lax.dot_general(a, b, (((1,), (0,)), ((), ())), preferred_element_type=F32)


def split3(x):
    hi = x.astype(BF16)
    rest = x - hi.astype(F32)
    mid = rest.astype(BF16)
    low = (rest - mid.astype(F32)).astype(BF16)
    return hi, mid, low


def eye_mask():
    return lax.broadcasted_iota(jnp.int32, (B, B), 0) == lax.broadcasted_iota(
        jnp.int32, (B, B), 1
    )


def gram_kernel(slot, parts, w_ref, d_ref, out_ref, scaled_ref, g_ref):
    rows = w_ref.shape[1]
    scale = d_ref[...].astype(F32)[slot : slot + 1]
    for i in range(rows // B):
        at = slice(i * B, (i + 1) * B)
        scaled_ref[at, :] = (w_ref[0, at, :].astype(F32) * scale).astype(BF16)
    for i in range(rows // B):
        at = slice(i * B, (i + 1) * B)
        g_ref[at, :] = lax.dot_general(
            scaled_ref[at, :], w_ref[0], (((1,), (1,)), ((), ())), preferred_element_type=F32
        )
    step = B // parts
    for b, (i, j) in enumerate(blocks_of(rows)):
        blk = g_ref[i * B : (i + 1) * B, j * B : (j + 1) * B]
        if i != j:
            blk = 0.5 * (blk + g_ref[j * B : (j + 1) * B, i * B : (i + 1) * B].T)
        for z in range(parts):
            out_ref[z, b * step : (b + 1) * step, :] = blk[z * step : (z + 1) * step, :]


def gram(slot, parts, matrices, ratios):
    _, rows, cols = matrices.shape
    height = len(blocks_of(rows)) * B // parts
    return pl.pallas_call(
        functools.partial(gram_kernel, slot, parts),
        grid=(1,),
        in_specs=[
            pl.BlockSpec((1, rows, cols), lambda i: (slot, 0, 0)),
            pl.BlockSpec(ratios.shape, lambda i: (0, 0)),
        ],
        out_specs=pl.BlockSpec((parts, height, B), lambda i: (0, 0, 0)),
        out_shape=jax.ShapeDtypeStruct((parts, height, B), F32),
        scratch_shapes=[pltpu.VMEM((rows, cols), BF16), pltpu.VMEM((rows, rows), F32)],
        name=f"gram{slot}",
    )(matrices, ratios)


def cg_block(parts_of_matrix, x_ref, r_ref, p_ref, rr_ref, bb_ref):
    hi, mid, low = parts_of_matrix
    n = x_ref.shape[1]

    def apply(p):
        ph, pm, plow = split3(p)
        a = mm(hi[...], jnp.concatenate([ph, pm, plow], axis=1))
        c = mm(mid[...], jnp.concatenate([ph, pm], axis=1))
        e = mm(low[...], ph)
        small = a[:, 2 * n :] + c[:, n:] + e
        return a[:, :n] + ((a[:, n : 2 * n] + c[:, :n]) + small)

    def body(carry):
        k, _ = carry
        p = p_ref[...]
        q = apply(p)
        rr = rr_ref[...]
        pq = jnp.sum(p * q, axis=0, keepdims=True)
        alpha = jnp.where(pq > 0.0, rr / jnp.where(pq > 0.0, pq, 1.0), 0.0)
        x_ref[...] += alpha * p
        r = r_ref[...] - alpha * q
        r_ref[...] = r
        new = jnp.sum(r * r, axis=0, keepdims=True)
        beta = jnp.where(rr > 0.0, new / jnp.where(rr > 0.0, rr, 1.0), 0.0)
        p_ref[...] = r + beta * p
        rr_ref[...] = new
        return k + 1, jnp.max(new - TOL2 * bb_ref[...])

    rhs = r_ref[...]
    x_ref[...] = jnp.zeros_like(rhs)
    p_ref[...] = rhs
    first = jnp.sum(rhs * rhs, axis=0, keepdims=True)
    rr_ref[...] = first
    bb_ref[...] = first
    lax.while_loop(
        lambda c: (c[0] < MAX_STEPS) & (c[1] > 0.0), body, (jnp.int32(0), jnp.max(first))
    )


def solve_kernel(
    recv_ref, reg_ref, rhs_ref, link_ref, g_ref, out_ref,
    hi_ref, mid_ref, low_ref, x_ref, r_ref, p_ref, rr_ref, bb_ref,
):
    parts = recv_ref.shape[0]
    rows = g_ref.shape[0]
    step = B // parts
    eye = eye_mask()
    for b, (i, j) in enumerate(blocks_of(rows)):
        ri, rj = slice(i * B, (i + 1) * B), slice(j * B, (j + 1) * B)
        for z in range(parts):
            g_ref[i * B + z * step : i * B + (z + 1) * step, rj] = recv_ref[
                z, b * step : (b + 1) * step, :
            ]
        blk = g_ref[ri, rj]
        if i == j:
            g_ref[ri, rj] = 0.5 * (blk + blk.T) + jnp.where(eye, reg_ref[:, rj], 0.0)
        else:
            g_ref[rj, ri] = blk.T
    for i in range(rows // B):
        at = slice(i * B, (i + 1) * B)
        hi_ref[at, :], mid_ref[at, :], low_ref[at, :] = split3(g_ref[at, :])
    r_ref[...] = rhs_ref[...].astype(F32)
    cg_block((hi_ref, mid_ref, low_ref), x_ref, r_ref, p_ref, rr_ref, bb_ref)
    n = x_ref.shape[1]
    pieces = jnp.concatenate(split3(x_ref[...]), axis=1)
    y = lax.dot_general(
        link_ref[...], pieces, (((0,), (0,)), ((), ())), preferred_element_type=F32
    )
    out_ref[...] = y[:, :n] + (y[:, n : 2 * n] + y[:, 2 * n :])


def solve(received, reg_row, rhs, link):
    rows, width = rhs.shape
    n0 = link.shape[1]
    return pl.pallas_call(
        solve_kernel,
        out_shape=(
            jax.ShapeDtypeStruct((rows, rows), F32),
            jax.ShapeDtypeStruct((n0, width), F32),
        ),
        scratch_shapes=[pltpu.VMEM((rows, rows), BF16)] * 3
        + [pltpu.VMEM((rows, width), F32)] * 3
        + [pltpu.VMEM((1, width), F32)] * 2,
        name="solve",
    )(received, reg_row, rhs, link)


def as_row(col, eye):
    return jnp.sum(jnp.where(eye, col, 0.0), axis=0, keepdims=True)


def times_row(mat_ref, row, eye):
    rows, cols = mat_ref.shape[0], row.shape[1]
    out = []
    for i in range(rows // B):
        part = mat_ref[i * B : (i + 1) * B, :cols].astype(F32) * row
        out.append(as_row(jnp.sum(part, axis=1, keepdims=True), eye))
    return jnp.concatenate(out, axis=1)


def cg_row(mat_ref, rhs, x_ref, r_ref, p_ref, eye):
    def body(carry):
        k, rr, stop = carry
        p = p_ref[...]
        q = times_row(mat_ref, p, eye)
        pq = jnp.sum(p * q)
        alpha = jnp.where(pq > 0.0, rr / jnp.where(pq > 0.0, pq, 1.0), 0.0)
        x_ref[...] += alpha * p
        r = r_ref[...] - alpha * q
        r_ref[...] = r
        new = jnp.sum(r * r)
        beta = jnp.where(rr > 0.0, new / jnp.where(rr > 0.0, rr, 1.0), 0.0)
        p_ref[...] = r + beta * p
        return k + 1, new, stop

    x_ref[...] = jnp.zeros_like(rhs)
    r_ref[...] = rhs
    p_ref[...] = rhs
    first = jnp.sum(rhs * rhs)
    lax.while_loop(
        lambda c: (c[0] < MAX_STEPS) & (c[1] > c[2]), body, (jnp.int32(0), first, TOL2 * first)
    )
    return x_ref[...]


def main_kernel(
    recv_ref, q_ref, c_ref, g_ref, link_ref, b_ref, first_ref, dual_ref,
    s_ref, x_ref, r_ref, p_ref,
):
    pair, count, each, _ = recv_ref.shape
    n0 = q_ref.shape[1]
    eye = eye_mask()
    for i in range(count):
        for k in range(pair):
            at = (i * pair + k) * each
            s_ref[at : at + each, :] = recv_ref[k, i]
    rho = []
    for i in range(n0 // B):
        at = slice(i * B, (i + 1) * B)
        rho.append(as_row(s_ref[at, n0 : n0 + 1], eye))
        s_ref[at, at] += jnp.where(eye, q_ref[:, at], 0.0)
    rhs = c_ref[...] - jnp.concatenate(rho, axis=1)
    first = cg_row(s_ref.at[:, :n0], rhs, x_ref, r_ref, p_ref, eye)
    first_ref[...] = first
    pushed = b_ref[...] + times_row(link_ref, first, eye)
    dual_ref[...] = cg_row(g_ref, pushed, x_ref, r_ref, p_ref, eye)


def main_solve(received, q_row, c_row, g, link, b_row):
    n0, rows = q_row.shape[1], b_row.shape[1]
    return pl.pallas_call(
        main_kernel,
        out_shape=(
            jax.ShapeDtypeStruct((1, n0), F32),
            jax.ShapeDtypeStruct((1, rows), F32),
        ),
        scratch_shapes=[pltpu.VMEM((n0, received.shape[-1]), F32)]
        + [pltpu.VMEM((1, n0), F32)] * 3,
        name="main_solve",
    )(received, q_row, c_row, g, link, b_row)


def primal_kernel(w_ref, d_ref, dual_ref, out_ref):
    for slot in range(w_ref.shape[0]):
        low = dual_ref[slot : slot + 1, :].astype(BF16)
        out_ref[slot : slot + 1, :] = d_ref[...].astype(F32)[slot : slot + 1] * mm(
            low, w_ref[slot]
        )


def primal(matrices, ratios, duals):
    return pl.pallas_call(
        primal_kernel,
        out_shape=jax.ShapeDtypeStruct(ratios.shape, F32),
        name="primal",
    )(matrices, ratios, duals)


def local(
    scen_size, col_size, matrices, ratios, damping, coupler, bounds, q_diag, c_vec, tallies
):
    n_s, n_z = scen_size, col_size
    rows = matrices.shape[1]
    n0 = coupler.shape[2]
    pos = lax.axis_index("scen")
    zpos = lax.axis_index("col")
    held = tallies[pos]
    before = tallies[jnp.maximum(pos - 1, 0)]
    own = held >= 1
    live = own | ((pos % 4 != 0) & (before == 2))
    forth = [(4 * b + i, 4 * b + i + 1) for b in range(n_s // 4) for i in range(3)]
    back = [(j, i) for i, j in forth]

    def everyone(x, axis, count, **kw):
        return lax.all_to_all(
            jnp.broadcast_to(x[None], (count,) + x.shape), axis, 0, 0, **kw
        )

    sides = [
        jnp.concatenate([coupler[k], damping[k : k + 1], bounds[k : k + 1]], axis=0)
        for k in range(2)
    ]
    side_moved = lax.ppermute(sides[1], "scen", forth)
    gram1 = gram(1, n_z, matrices, ratios)
    gram_moved = lax.ppermute(gram1, "scen", forth)
    gram0 = gram(0, n_z, matrices, ratios)
    side = jnp.where(own, sides[0], side_moved)
    link = side[:rows]
    reg_row = side[rows : rows + 1].astype(F32)
    b_row = side[rows + 1 : rows + 2].astype(F32)
    share = n0 // n_z
    width = -(-(share + 1) // B) * B
    rhs = jnp.concatenate(
        [
            lax.dynamic_slice(link, (0, zpos * share), (rows, share)),
            side[rows + 1][:, None],
            jnp.zeros((rows, width - share - 1), BF16),
        ],
        axis=1,
    )
    rhs = jnp.where(live, rhs, jnp.zeros_like(rhs))

    partial = jnp.where(own, gram0, gram_moved)
    shard = jnp.sum(lax.all_to_all(partial, "col", 0, 0), axis=0)
    g, terms = solve(everyone(shard, "col", n_z), reg_row, rhs, link)

    each = n0 // n_s
    mine = jnp.sum(lax.all_to_all(terms.reshape(n_s, each, width), "scen", 0, 0), axis=0)
    wide = everyone(mine, "col", n_z)
    flat = jnp.concatenate(
        [wide[k, :, :share] for k in range(n_z)] + [wide[0, :, share : share + B]], axis=1
    )
    if flat.shape[1] < n0 + B:
        flat = jnp.pad(flat, ((0, 0), (0, n0 + B - flat.shape[1])))
    same = [[2 * i + k for i in range(n_s // 2)] for k in range(2)]
    cores = [[2 * i, 2 * i + 1] for i in range(n_s // 2)]
    half = everyone(flat, "scen", n_s // 2, axis_index_groups=same)
    full = everyone(half, "scen", 2, axis_index_groups=cores)
    first, dual = main_solve(full, q_diag[None], c_vec[None], g, link, b_row)

    returned = lax.ppermute(dual, "scen", back)
    duals = jnp.concatenate(
        [
            jnp.where(own, dual, jnp.zeros_like(dual)),
            jnp.where(held >= 2, returned, jnp.zeros_like(dual)),
        ],
        axis=0,
    )
    return first[0], duals, primal(matrices, ratios, duals)


def solution(mesh):
    body = functools.partial(local, mesh.shape["scen"], mesh.shape["col"])
    return jax.shard_map(
        body,
        mesh=mesh,
        in_specs=(
            P("scen", None, "col"),
            P("scen", "col"),
            P("scen", None),
            P("scen", None, None),
            P("scen", None),
            P(),
            P(),
            P(),
        ),
        out_specs=(P(), P("scen", None), P("scen", "col")),
        check_vma=False,
    )
```

```python
import functools

import jax
import jax.numpy as jnp
from jax import lax
from jax.experimental import pallas as pl
from jax.experimental.pallas import tpu as pltpu
from jax.sharding import PartitionSpec as P

F32 = jnp.float32
BF16 = jnp.bfloat16
B = 128
TOL2 = 1e-12
MAX_STEPS = 4096
VMEM = 20 * 2**20


def blocks_of(rows):
    n = rows // B
    return [(i, j) for i in range(n) for j in range(i + 1)]


def mm(a, b):
    return lax.dot_general(a, b, (((1,), (0,)), ((), ())), preferred_element_type=F32)


def split3(x):
    hi = x.astype(BF16)
    rest = x - hi.astype(F32)
    mid = rest.astype(BF16)
    low = (rest - mid.astype(F32)).astype(BF16)
    return hi, mid, low


def eye_mask():
    return lax.broadcasted_iota(jnp.int32, (B, B), 0) == lax.broadcasted_iota(
        jnp.int32, (B, B), 1
    )


def gram_kernel(slot, parts, w_ref, d_ref, out_ref, scaled_ref, g_ref):
    rows = w_ref.shape[1]
    scale = d_ref[...].astype(F32)[slot : slot + 1]
    for i in range(rows // B):
        at = slice(i * B, (i + 1) * B)
        scaled_ref[at, :] = (w_ref[0, at, :].astype(F32) * scale).astype(BF16)
    for i in range(rows // B):
        at = slice(i * B, (i + 1) * B)
        g_ref[at, :] = lax.dot_general(
            scaled_ref[at, :], w_ref[0], (((1,), (1,)), ((), ())), preferred_element_type=F32
        )
    step = B // parts
    for b, (i, j) in enumerate(blocks_of(rows)):
        blk = g_ref[i * B : (i + 1) * B, j * B : (j + 1) * B]
        if i != j:
            blk = 0.5 * (blk + g_ref[j * B : (j + 1) * B, i * B : (i + 1) * B].T)
        for z in range(parts):
            out_ref[z, b * step : (b + 1) * step, :] = blk[z * step : (z + 1) * step, :]


def gram(slot, parts, matrices, ratios):
    _, rows, cols = matrices.shape
    height = len(blocks_of(rows)) * B // parts
    return pl.pallas_call(
        functools.partial(gram_kernel, slot, parts),
        grid=(1,),
        in_specs=[
            pl.BlockSpec((1, rows, cols), lambda i: (slot, 0, 0)),
            pl.BlockSpec(ratios.shape, lambda i: (0, 0)),
        ],
        out_specs=pl.BlockSpec((parts, height, B), lambda i: (0, 0, 0)),
        out_shape=jax.ShapeDtypeStruct((parts, height, B), F32),
        scratch_shapes=[pltpu.VMEM((rows, cols), BF16), pltpu.VMEM((rows, rows), F32)],
        compiler_params=pltpu.CompilerParams(vmem_limit_bytes=VMEM),
        name=f"gram{slot}",
    )(matrices, ratios)


def ratio(a, b):
    ok = b > 0.0
    return jnp.where(ok, a / jnp.where(ok, b, 1.0), 0.0)


def low_lanes(shape):
    return lax.broadcasted_iota(jnp.int32, shape, len(shape) - 1) < B // 2


def cg_block(pieces, x_ref, r_ref, p_ref, s_ref, rb_ref, sc_ref):
    hi, mid = pieces
    rows = x_ref.shape[0]
    tiles = [slice(i * B, (i + 1) * B) for i in range(rows // B)]

    def body(carry):
        k, _ = carry
        rb = rb_ref[...]
        gamma, old, was, bound = (sc_ref[i : i + 1, :] for i in range(4))
        delta = jnp.zeros_like(gamma)
        for at in tiles:
            w = mm(hi[at, :], rb) + mm(mid[at, :], rb)
            x_ref[at, :] += was * p_ref[at, :]
            p_ref[at, :] = rb_ref[at, :].astype(F32) + ratio(gamma, old) * p_ref[at, :]
            s_ref[at, :] = w + ratio(gamma, old) * s_ref[at, :]
            delta += jnp.sum(p_ref[at, :] * s_ref[at, :], axis=0, keepdims=True)
        alpha = ratio(gamma, delta)
        new = jnp.zeros_like(gamma)
        size = jnp.zeros_like(gamma)
        for at in tiles:
            r = r_ref[at, :] - alpha * s_ref[at, :]
            r_ref[at, :] = r
            rounded = r.astype(BF16)
            rb_ref[at, :] = rounded
            new += jnp.sum(r * rounded.astype(F32), axis=0, keepdims=True)
        sc_ref[0:1, :] = new
        sc_ref[1:2, :] = gamma
        sc_ref[2:3, :] = alpha
        return k + 1, jnp.max(new - bound)

    rhs = r_ref[...]
    x_ref[...] = jnp.zeros_like(rhs)
    p_ref[...] = jnp.zeros_like(rhs)
    s_ref[...] = jnp.zeros_like(rhs)
    rounded = rhs.astype(BF16)
    rb_ref[...] = rounded
    first = jnp.sum(rhs * rounded.astype(F32), axis=0, keepdims=True)
    sc_ref[0:1, :] = first
    sc_ref[1:3, :] = jnp.zeros((2,) + first.shape[1:], F32)
    sc_ref[3:4, :] = TOL2 * first
    lax.while_loop(
        lambda c: (c[0] < MAX_STEPS) & (c[1] > 0.0), body, (jnp.int32(0), jnp.max(first))
    )
    for at in tiles:
        x_ref[at, :] += sc_ref[2:3, :] * p_ref[at, :]


def solve_kernel(
    recv_ref, reg_ref, rhs_ref, link_ref, g_ref, out_ref,
    hi_ref, mid_ref, x_ref, r_ref, p_ref, s_ref, rb_ref, sc_ref,
):
    parts = recv_ref.shape[0]
    rows = g_ref.shape[0]
    step = B // parts
    eye = eye_mask()
    for b, (i, j) in enumerate(blocks_of(rows)):
        ri, rj = slice(i * B, (i + 1) * B), slice(j * B, (j + 1) * B)
        blk = jnp.concatenate(
            [recv_ref[z, b * step : (b + 1) * step, :] for z in range(parts)], axis=0
        )
        other = blk.T
        if i == j:
            blk = 0.5 * (blk + other) + jnp.where(eye, reg_ref[:, rj], 0.0)
        g_ref[ri, rj] = blk
        hi_ref[ri, rj], mid_ref[ri, rj] = split3(blk)[:2]
        if i != j:
            g_ref[rj, ri] = other
            hi_ref[rj, ri], mid_ref[rj, ri] = split3(other)[:2]
    r_ref[...] = rhs_ref[...].astype(F32)
    cg_block((hi_ref, mid_ref), x_ref, r_ref, p_ref, s_ref, rb_ref, sc_ref)
    n = x_ref.shape[1]
    pieces = jnp.concatenate(split3(x_ref[...]), axis=1)
    y = lax.dot_general(
        link_ref[...], pieces, (((0,), (0,)), ((), ())), preferred_element_type=F32
    )
    y = y[:, :n] + (y[:, n : 2 * n] + y[:, 2 * n :])
    half, quarter = B // 2, B // 4
    after = lax.rem(lax.axis_index("col") + 1, n0_blocks(rows))
    row = lax.broadcasted_iota(jnp.int32, y.shape, 0)
    lane = lax.broadcasted_iota(jnp.int32, y.shape, 1)
    start = after * half
    here = (row >= start) & (row < start + half) & (lane == 0)
    x_ref[...] = jnp.where(here, pltpu.roll(y, half, 1), y)
    low = low_lanes((quarter, B))
    for t in range(rows // B):
        for c in range(2):
            at = t * B + c * quarter
            up = pltpu.roll(x_ref[at + half : at + half + quarter, :], half, 1)
            out_ref[c, :, t, :] = jnp.where(low, x_ref[at : at + quarter, :], up)


def n0_blocks(rows):
    return rows // (B // 2)


def solve(received, reg_row, rhs, link):
    rows, width = rhs.shape
    return pl.pallas_call(
        solve_kernel,
        out_shape=(
            jax.ShapeDtypeStruct((rows, rows), F32),
            jax.ShapeDtypeStruct((2, B // 4, rows // B, B), F32),
        ),
        scratch_shapes=[pltpu.VMEM((rows, rows), BF16)] * 2
        + [pltpu.VMEM((rows, width), F32)] * 4
        + [pltpu.VMEM((rows, width), BF16), pltpu.VMEM((8, width), F32)],
        compiler_params=pltpu.CompilerParams(vmem_limit_bytes=VMEM),
        name="solve",
    )(received, reg_row, rhs, link)


def as_row(col, eye):
    return jnp.sum(jnp.where(eye, col, 0.0), axis=0, keepdims=True)


def as_col(row, eye):
    return jnp.sum(jnp.where(eye, row, 0.0), axis=1, keepdims=True)


def times_row(mat_ref, row, eye):
    rows = mat_ref.shape[0]
    out = []
    for i in range(rows // B):
        part = mat_ref[i * B : (i + 1) * B, :].astype(F32) * row
        out.append(as_row(jnp.sum(part, axis=1, keepdims=True), eye))
    return jnp.concatenate(out, axis=1)


def sym_times_row(mat_ref, row, eye):
    total = None
    for i in range(mat_ref.shape[0] // B):
        at = slice(i * B, (i + 1) * B)
        part = jnp.sum(mat_ref[at, :] * as_col(row[:, at], eye), axis=0, keepdims=True)
        total = part if total is None else total + part
    return total


def lane_sum(row):
    return jnp.sum(row, axis=1, keepdims=True)


def cg_row(mat_ref, rhs, x_ref, r_ref, p_ref, s_ref, sc_ref, eye):
    def body(carry):
        k, _ = carry
        gamma, old, bound = (sc_ref[i : i + 1, 0:1] for i in range(3))
        r = r_ref[...]
        w = sym_times_row(mat_ref, r, eye)
        beta = ratio(gamma, old)
        p = r + beta * p_ref[...]
        s = w + beta * s_ref[...]
        alpha = ratio(gamma, lane_sum(p * s))
        p_ref[...] = p
        s_ref[...] = s
        x_ref[...] += alpha * p
        r = r - alpha * s
        r_ref[...] = r
        new = lane_sum(r * r)
        sc_ref[0:1, 0:1] = new
        sc_ref[1:2, 0:1] = gamma
        return k + 1, jnp.max(new - bound)

    zero = jnp.zeros_like(rhs)
    x_ref[...] = zero
    p_ref[...] = zero
    s_ref[...] = zero
    r_ref[...] = rhs
    first = lane_sum(rhs * rhs)
    sc_ref[0:1, 0:1] = first
    sc_ref[1:2, 0:1] = jnp.zeros_like(first)
    sc_ref[2:3, 0:1] = TOL2 * first
    lax.while_loop(
        lambda c: (c[0] < MAX_STEPS) & (c[1] > 0.0), body, (jnp.int32(0), jnp.max(first))
    )
    return x_ref[...]


def main_kernel(
    mine_ref, other_ref, q_ref, c_ref, g_ref, link_ref, b_ref, first_ref, dual_ref,
    m_ref, x_ref, r_ref, p_ref, s_ref, sc_ref,
):
    quarter, shards, tiles, _ = mine_ref.shape
    half = 2 * quarter
    eye = eye_mask()
    core = lax.rem(lax.axis_index("scen"), 2)
    low = low_lanes((quarter, B))
    for src, which in ((mine_ref, core), (other_ref, 1 - core)):
        for t in range(tiles):
            top = pl.multiple_of(which * quarter + t * B, quarter)
            for m in range(shards // 2):
                v0, v1 = src[:, 2 * m, t, :], src[:, 2 * m + 1, t, :]
                at = slice(m * B, (m + 1) * B)
                m_ref[pl.ds(top, quarter), at] = jnp.where(low, v0, pltpu.roll(v1, half, 1))
                m_ref[pl.ds(top + half, quarter), at] = jnp.where(
                    low, pltpu.roll(v0, half, 1), v1
                )
    row = lax.broadcasted_iota(jnp.int32, (B, B), 0)
    lane = lax.broadcasted_iota(jnp.int32, (B, B), 1)
    rho = []
    for t in range(tiles):
        at = slice(t * B, (t + 1) * B)
        e = (t + tiles - 1) % tiles
        before = slice(e * B, (e + 1) * B)
        near, far = m_ref[at, at], m_ref[at, before]
        rho.append(as_row(jnp.where(row[:, :1] < half, far[:, half : half + 1], near[:, :1]), eye))
        give = jnp.where(
            lane[:1] < half,
            m_ref[e * B + half : e * B + half + 1, at],
            m_ref[t * B : t * B + 1, at],
        )
        give = as_col(give, eye)
        m_ref[at, at] = jnp.where((row >= half) & (lane == 0), give, near) + jnp.where(
            eye, q_ref[:, at], 0.0
        )
        m_ref[at, before] = jnp.where((row < half) & (lane == half), give, far)
    rhs = c_ref[...] - jnp.concatenate(rho, axis=1)
    refs = (x_ref, r_ref, p_ref, s_ref, sc_ref)
    first = cg_row(m_ref, rhs, *refs, eye)
    first_ref[...] = first
    pushed = b_ref[...] + times_row(link_ref, first, eye)
    dual_ref[...] = cg_row(g_ref, pushed, *refs, eye)


def main_solve(mine, other, q_row, c_row, g, link, b_row):
    n0, rows = q_row.shape[1], b_row.shape[1]
    return pl.pallas_call(
        main_kernel,
        out_shape=(
            jax.ShapeDtypeStruct((1, n0), F32),
            jax.ShapeDtypeStruct((1, rows), F32),
        ),
        scratch_shapes=[pltpu.VMEM((n0, n0), F32)]
        + [pltpu.VMEM((1, n0), F32)] * 4
        + [pltpu.VMEM((8, B), F32)],
        compiler_params=pltpu.CompilerParams(vmem_limit_bytes=VMEM),
        name="main_solve",
    )(mine, other, q_row, c_row, g, link, b_row)


def primal_kernel(tallies_ref, w_ref, d_ref, dual_ref, back_ref, y_ref, out_ref):
    held = tallies_ref[lax.axis_index("scen")]
    scale = d_ref[...].astype(F32)
    for slot, source in enumerate((dual_ref, back_ref)):
        dual = source[...]
        dual = jnp.where(held > slot, dual, jnp.zeros_like(dual))
        y_ref[slot : slot + 1, :] = dual
        out_ref[slot : slot + 1, :] = scale[slot : slot + 1] * mm(
            dual.astype(BF16), w_ref[slot]
        )


def primal(tallies, matrices, ratios, dual, back):
    return pl.pallas_call(
        primal_kernel,
        in_specs=[pl.BlockSpec(memory_space=pltpu.SMEM)]
        + [pl.BlockSpec(memory_space=pltpu.VMEM)] * 4,
        out_shape=(
            jax.ShapeDtypeStruct((2, dual.shape[1]), F32),
            jax.ShapeDtypeStruct(ratios.shape, F32),
        ),
        compiler_params=pltpu.CompilerParams(vmem_limit_bytes=VMEM),
        name="primal",
    )(tallies, matrices, ratios, dual, back)


def local(
    scen_size, col_size, matrices, ratios, damping, coupler, bounds, q_diag, c_vec, tallies
):
    n_s, n_z = scen_size, col_size
    rows = matrices.shape[1]
    n0 = coupler.shape[2]
    pos = lax.axis_index("scen")
    zpos = lax.axis_index("col")
    held = tallies[pos]
    before = tallies[jnp.maximum(pos - 1, 0)]
    own = held >= 1
    live = own | ((pos % 4 != 0) & (before == 2))
    forth = [(4 * b + i, 4 * b + i + 1) for b in range(n_s // 4) for i in range(3)]
    back = [(j, i) for i, j in forth]

    def everyone(x, axis, count, **kw):
        return lax.all_to_all(
            jnp.broadcast_to(x[None], (count,) + x.shape), axis, 0, 0, **kw
        )

    sides = [
        jnp.concatenate([coupler[k], damping[k : k + 1], bounds[k : k + 1]], axis=0)
        for k in range(2)
    ]
    side_moved = lax.ppermute(sides[1], "scen", forth)
    gram1 = gram(1, n_z, matrices, ratios)
    gram_moved = lax.ppermute(gram1, "scen", forth)
    gram0 = gram(0, n_z, matrices, ratios)
    side = jnp.where(own, sides[0], side_moved)
    link = side[:rows]
    reg_row = side[rows : rows + 1].astype(F32)
    b_row = side[rows + 1 : rows + 2].astype(F32)
    share = n0 // n_z
    width = -(-(share + 1) // B) * B
    rhs = jnp.concatenate(
        [
            lax.dynamic_slice(link, (0, zpos * share), (rows, share)),
            side[rows + 1][:, None],
            jnp.zeros((rows, width - share - 1), BF16),
        ],
        axis=1,
    )
    rhs = jnp.where(live, rhs, jnp.zeros_like(rhs))

    partial = jnp.where(own, gram0, gram_moved)
    shard = jnp.sum(lax.all_to_all(partial, "col", 0, 0), axis=0)
    g, terms = solve(everyone(shard, "col", n_z), reg_row, rhs, link)

    count = n_s // 2
    same = [[2 * i + k for i in range(count)] for k in range(2)]
    terms = terms.reshape((n_s,) + terms.shape[2:])
    mine = lax.all_to_all(terms, "scen", 0, 0, axis_index_groups=[same[0] + same[1]])
    wide = everyone(jnp.sum(mine, axis=0), "col", n_z)
    half = everyone(wide, "scen", count, axis_index_groups=same)
    other = lax.ppermute(half, "scen", [(i, i ^ 1) for i in range(n_s)])
    first, dual = main_solve(half, other, q_diag[None], c_vec[None], g, link, b_row)

    returned = lax.ppermute(dual, "scen", back)
    duals, primals = primal(tallies, matrices, ratios, dual, returned)
    return first[0], duals, primals


def solution(mesh):
    body = functools.partial(local, mesh.shape["scen"], mesh.shape["col"])
    return jax.shard_map(
        body,
        mesh=mesh,
        in_specs=(
            P("scen", None, "col"),
            P("scen", "col"),
            P("scen", None),
            P("scen", None, None),
            P("scen", None),
            P(),
            P(),
            P(),
        ),
        out_specs=(P(), P("scen", None), P("scen", "col")),
        check_vma=False,
    )
```

```python
import functools

import jax
import jax.numpy as jnp
from jax import lax
from jax.experimental import pallas as pl
from jax.experimental.pallas import tpu as pltpu
from jax.sharding import PartitionSpec as P

F32 = jnp.float32
BF16 = jnp.bfloat16
B = 128
TOL2 = 1e-11
MAX_STEPS = 4096
VMEM = 20 * 2**20


def blocks_of(rows):
    n = rows // B
    return [(i, j) for i in range(n) for j in range(i + 1)]


def mm(a, b):
    return lax.dot_general(a, b, (((1,), (0,)), ((), ())), preferred_element_type=F32)


def split3(x):
    hi = x.astype(BF16)
    rest = x - hi.astype(F32)
    mid = rest.astype(BF16)
    low = (rest - mid.astype(F32)).astype(BF16)
    return hi, mid, low


def eye_mask():
    return lax.broadcasted_iota(jnp.int32, (B, B), 0) == lax.broadcasted_iota(
        jnp.int32, (B, B), 1
    )


def gram_kernel(slot, parts, w_hbm, d_hbm, out_ref, w_ref, d_ref, scaled_ref, g_ref, sem):
    rows = w_ref.shape[0]
    tiles = [slice(i * B, (i + 1) * B) for i in range(rows // B)]
    scale_copy = pltpu.make_async_copy(d_hbm, d_ref, sem.at[len(tiles)])
    copies = [
        pltpu.make_async_copy(w_hbm.at[slot, at, :], w_ref.at[at, :], sem.at[i])
        for i, at in enumerate(tiles)
    ]
    scale_copy.start()
    for copy in copies:
        copy.start()
    scale_copy.wait()
    scale = d_ref[...].astype(F32)[slot : slot + 1]
    for at, copy in zip(tiles, copies):
        copy.wait()
        scaled_ref[at, :] = (w_ref[at, :].astype(F32) * scale).astype(BF16)
    for at in tiles:
        g_ref[at, :] = lax.dot_general(
            scaled_ref[at, :], w_ref[...], (((1,), (1,)), ((), ())), preferred_element_type=F32
        )
    step = B // parts
    for b, (i, j) in enumerate(blocks_of(rows)):
        blk = g_ref[tiles[i], tiles[j]]
        if i != j:
            blk = 0.5 * (blk + g_ref[tiles[j], tiles[i]].T)
        for z in range(parts):
            out_ref[z, b * step : (b + 1) * step, :] = blk[z * step : (z + 1) * step, :]


def gram(slot, parts, matrices, ratios):
    _, rows, cols = matrices.shape
    height = len(blocks_of(rows)) * B // parts
    return pl.pallas_call(
        functools.partial(gram_kernel, slot, parts),
        in_specs=[pl.BlockSpec(memory_space=pl.ANY)] * 2,
        out_shape=jax.ShapeDtypeStruct((parts, height, B), F32),
        scratch_shapes=[
            pltpu.VMEM((rows, cols), BF16),
            pltpu.VMEM(ratios.shape, BF16),
            pltpu.VMEM((rows, cols), BF16),
            pltpu.VMEM((rows, rows), F32),
            pltpu.SemaphoreType.DMA((rows // B + 1,)),
        ],
        compiler_params=pltpu.CompilerParams(vmem_limit_bytes=VMEM),
        name=f"gram{slot}",
    )(matrices, ratios)


def ratio(a, b):
    ok = b > 0.0
    return jnp.where(ok, a / jnp.where(ok, b, 1.0), 0.0)


def low_lanes(shape):
    return lax.broadcasted_iota(jnp.int32, shape, len(shape) - 1) < B // 2


def cg_block(pieces, x_ref, r_ref, p_ref, s_ref, rb_ref, sc_ref):
    hi, mid = pieces
    rows = x_ref.shape[0]
    tiles = [slice(i * B, (i + 1) * B) for i in range(rows // B)]

    def body(carry):
        k, _ = carry
        rb = rb_ref[...]
        gamma, old, was, bound = (sc_ref[i : i + 1, :] for i in range(4))
        delta = jnp.zeros_like(gamma)
        for at in tiles:
            w = mm(hi[at, :], rb) + mm(mid[at, :], rb)
            x_ref[at, :] += was * p_ref[at, :]
            p_ref[at, :] = rb_ref[at, :].astype(F32) + ratio(gamma, old) * p_ref[at, :]
            s_ref[at, :] = w + ratio(gamma, old) * s_ref[at, :]
            delta += jnp.sum(p_ref[at, :] * s_ref[at, :], axis=0, keepdims=True)
        alpha = ratio(gamma, delta)
        new = jnp.zeros_like(gamma)
        size = jnp.zeros_like(gamma)
        for at in tiles:
            r = r_ref[at, :] - alpha * s_ref[at, :]
            r_ref[at, :] = r
            rounded = r.astype(BF16)
            rb_ref[at, :] = rounded
            new += jnp.sum(r * rounded.astype(F32), axis=0, keepdims=True)
        sc_ref[0:1, :] = new
        sc_ref[1:2, :] = gamma
        sc_ref[2:3, :] = alpha
        return k + 1, jnp.max(gamma - bound)

    rhs = r_ref[...]
    x_ref[...] = jnp.zeros_like(rhs)
    p_ref[...] = jnp.zeros_like(rhs)
    s_ref[...] = jnp.zeros_like(rhs)
    rounded = rhs.astype(BF16)
    rb_ref[...] = rounded
    first = jnp.sum(rhs * rounded.astype(F32), axis=0, keepdims=True)
    sc_ref[0:1, :] = first
    sc_ref[1:3, :] = jnp.zeros((2,) + first.shape[1:], F32)
    sc_ref[3:4, :] = TOL2 * first
    lax.while_loop(
        lambda c: (c[0] < MAX_STEPS) & (c[1] > 0.0), body, (jnp.int32(0), jnp.max(first))
    )
    for at in tiles:
        x_ref[at, :] += sc_ref[2:3, :] * p_ref[at, :]


def solve_kernel(
    recv_ref, reg_ref, rhs_ref, link_ref, g_ref, out_ref,
    hi_ref, mid_ref, x_ref, r_ref, p_ref, s_ref, rb_ref, sc_ref,
):
    parts = recv_ref.shape[0]
    rows = g_ref.shape[0]
    step = B // parts
    eye = eye_mask()
    for b, (i, j) in enumerate(blocks_of(rows)):
        ri, rj = slice(i * B, (i + 1) * B), slice(j * B, (j + 1) * B)
        blk = jnp.concatenate(
            [recv_ref[z, b * step : (b + 1) * step, :] for z in range(parts)], axis=0
        )
        other = blk.T
        if i == j:
            blk = 0.5 * (blk + other) + jnp.where(eye, reg_ref[:, rj], 0.0)
        g_ref[ri, rj] = blk
        hi_ref[ri, rj], mid_ref[ri, rj] = split3(blk)[:2]
        if i != j:
            g_ref[rj, ri] = other
            hi_ref[rj, ri], mid_ref[rj, ri] = split3(other)[:2]
    r_ref[...] = rhs_ref[...].astype(F32)
    cg_block((hi_ref, mid_ref), x_ref, r_ref, p_ref, s_ref, rb_ref, sc_ref)
    n = x_ref.shape[1]
    pieces = jnp.concatenate(split3(x_ref[...]), axis=1)
    y = lax.dot_general(
        link_ref[...], pieces, (((0,), (0,)), ((), ())), preferred_element_type=F32
    )
    y = y[:, :n] + (y[:, n : 2 * n] + y[:, 2 * n :])
    half, quarter = B // 2, B // 4
    after = lax.rem(lax.axis_index("col") + 1, n0_blocks(rows))
    row = lax.broadcasted_iota(jnp.int32, y.shape, 0)
    lane = lax.broadcasted_iota(jnp.int32, y.shape, 1)
    start = after * half
    here = (row >= start) & (row < start + half) & (lane == 0)
    x_ref[...] = jnp.where(here, pltpu.roll(y, half, 1), y)
    low = low_lanes((quarter, B))
    for t in range(rows // B):
        for c in range(2):
            at = t * B + c * quarter
            up = pltpu.roll(x_ref[at + half : at + half + quarter, :], half, 1)
            out_ref[c, :, t, :] = jnp.where(low, x_ref[at : at + quarter, :], up)


def n0_blocks(rows):
    return rows // (B // 2)


def solve(received, reg_row, rhs, link):
    rows, width = rhs.shape
    return pl.pallas_call(
        solve_kernel,
        out_shape=(
            jax.ShapeDtypeStruct((rows, rows), F32),
            jax.ShapeDtypeStruct((2, B // 4, rows // B, B), F32),
        ),
        scratch_shapes=[pltpu.VMEM((rows, rows), BF16)] * 2
        + [pltpu.VMEM((rows, width), F32)] * 4
        + [pltpu.VMEM((rows, width), BF16), pltpu.VMEM((8, width), F32)],
        compiler_params=pltpu.CompilerParams(vmem_limit_bytes=VMEM),
        name="solve",
    )(received, reg_row, rhs, link)


def as_row(col, eye):
    return jnp.sum(jnp.where(eye, col, 0.0), axis=0, keepdims=True)


def as_col(row, eye):
    return jnp.sum(jnp.where(eye, row, 0.0), axis=1, keepdims=True)


def times_row(mat_ref, row, eye):
    rows = mat_ref.shape[0]
    out = []
    for i in range(rows // B):
        part = mat_ref[i * B : (i + 1) * B, :].astype(F32) * row
        out.append(as_row(jnp.sum(part, axis=1, keepdims=True), eye))
    return jnp.concatenate(out, axis=1)


def sym_times_row(mat_ref, row, eye):
    total = None
    for i in range(mat_ref.shape[0] // B):
        at = slice(i * B, (i + 1) * B)
        part = jnp.sum(mat_ref[at, :] * as_col(row[:, at], eye), axis=0, keepdims=True)
        total = part if total is None else total + part
    return total


def lane_sum(row):
    return jnp.sum(row, axis=1, keepdims=True)


def cg_row(mat_ref, rhs, x_ref, r_ref, p_ref, s_ref, sc_ref, eye):
    def body(carry):
        k, _ = carry
        old, bound, scale = (sc_ref[i : i + 1, 0:1] for i in range(3))
        r = r_ref[...]
        gamma = lane_sum(r * r)
        w = sym_times_row(mat_ref, r, eye)
        delta = lane_sum(r * w)
        beta = ratio(gamma, old)
        alpha = ratio(gamma, delta - beta * gamma * scale)
        p = r + beta * p_ref[...]
        s = w + beta * s_ref[...]
        p_ref[...] = p
        s_ref[...] = s
        x_ref[...] += alpha * p
        r_ref[...] = r - alpha * s
        sc_ref[0:1, 0:1] = gamma
        sc_ref[2:3, 0:1] = ratio(jnp.ones_like(alpha), alpha)
        return k + 1, jnp.max(gamma - bound)

    zero = jnp.zeros_like(rhs)
    x_ref[...] = zero
    p_ref[...] = zero
    s_ref[...] = zero
    r_ref[...] = rhs
    first = lane_sum(rhs * rhs)
    sc_ref[0:1, 0:1] = jnp.zeros_like(first)
    sc_ref[1:2, 0:1] = TOL2 * first
    sc_ref[2:3, 0:1] = jnp.zeros_like(first)
    lax.while_loop(
        lambda c: (c[0] < MAX_STEPS) & (c[1] > 0.0), body, (jnp.int32(0), jnp.max(first))
    )
    return x_ref[...]


def main_kernel(
    mine_ref, other_ref, q_ref, c_ref, g_ref, link_ref, b_ref, first_ref, dual_ref,
    m_ref, x_ref, r_ref, p_ref, s_ref, sc_ref,
):
    quarter, shards, tiles, _ = mine_ref.shape
    half = 2 * quarter
    eye = eye_mask()
    core = lax.rem(lax.axis_index("scen"), 2)
    low = low_lanes((quarter, B))
    for src, which in ((mine_ref, core), (other_ref, 1 - core)):
        for t in range(tiles):
            top = pl.multiple_of(which * quarter + t * B, quarter)
            for m in range(shards // 2):
                v0, v1 = src[:, 2 * m, t, :], src[:, 2 * m + 1, t, :]
                at = slice(m * B, (m + 1) * B)
                m_ref[pl.ds(top, quarter), at] = jnp.where(low, v0, pltpu.roll(v1, half, 1))
                m_ref[pl.ds(top + half, quarter), at] = jnp.where(
                    low, pltpu.roll(v0, half, 1), v1
                )
    row = lax.broadcasted_iota(jnp.int32, (B, B), 0)
    lane = lax.broadcasted_iota(jnp.int32, (B, B), 1)
    rho = []
    for t in range(tiles):
        at = slice(t * B, (t + 1) * B)
        e = (t + tiles - 1) % tiles
        before = slice(e * B, (e + 1) * B)
        near, far = m_ref[at, at], m_ref[at, before]
        rho.append(as_row(jnp.where(row[:, :1] < half, far[:, half : half + 1], near[:, :1]), eye))
        give = jnp.where(
            lane[:1] < half,
            m_ref[e * B + half : e * B + half + 1, at],
            m_ref[t * B : t * B + 1, at],
        )
        give = as_col(give, eye)
        m_ref[at, at] = jnp.where((row >= half) & (lane == 0), give, near) + jnp.where(
            eye, q_ref[:, at], 0.0
        )
        m_ref[at, before] = jnp.where((row < half) & (lane == half), give, far)
    rhs = c_ref[...] - jnp.concatenate(rho, axis=1)
    refs = (x_ref, r_ref, p_ref, s_ref, sc_ref)
    first = cg_row(m_ref, rhs, *refs, eye)
    first_ref[...] = first
    pushed = b_ref[...] + times_row(link_ref, first, eye)
    dual_ref[...] = cg_row(g_ref, pushed, *refs, eye)


def main_solve(mine, other, q_row, c_row, g, link, b_row):
    n0, rows = q_row.shape[1], b_row.shape[1]
    return pl.pallas_call(
        main_kernel,
        out_shape=(
            jax.ShapeDtypeStruct((1, n0), F32),
            jax.ShapeDtypeStruct((1, rows), F32),
        ),
        scratch_shapes=[pltpu.VMEM((n0, n0), F32)]
        + [pltpu.VMEM((1, n0), F32)] * 4
        + [pltpu.VMEM((8, B), F32)],
        compiler_params=pltpu.CompilerParams(vmem_limit_bytes=VMEM),
        name="main_solve",
    )(mine, other, q_row, c_row, g, link, b_row)


def primal_kernel(tallies_ref, w_ref, d_ref, dual_ref, back_ref, y_ref, out_ref):
    held = tallies_ref[lax.axis_index("scen")]
    scale = d_ref[...].astype(F32)
    for slot, source in enumerate((dual_ref, back_ref)):
        dual = source[...]
        dual = jnp.where(held > slot, dual, jnp.zeros_like(dual))
        y_ref[slot : slot + 1, :] = dual
        out_ref[slot : slot + 1, :] = scale[slot : slot + 1] * mm(
            dual.astype(BF16), w_ref[slot]
        )


def primal(tallies, matrices, ratios, dual, back):
    return pl.pallas_call(
        primal_kernel,
        in_specs=[pl.BlockSpec(memory_space=pltpu.SMEM)]
        + [pl.BlockSpec(memory_space=pltpu.VMEM)] * 4,
        out_shape=(
            jax.ShapeDtypeStruct((2, dual.shape[1]), F32),
            jax.ShapeDtypeStruct(ratios.shape, F32),
        ),
        compiler_params=pltpu.CompilerParams(vmem_limit_bytes=VMEM),
        name="primal",
    )(tallies, matrices, ratios, dual, back)


def local(
    scen_size, col_size, matrices, ratios, damping, coupler, bounds, q_diag, c_vec, tallies
):
    n_s, n_z = scen_size, col_size
    rows = matrices.shape[1]
    n0 = coupler.shape[2]
    pos = lax.axis_index("scen")
    zpos = lax.axis_index("col")
    held = tallies[pos]
    own = held >= 1
    live = own | (tallies[pos ^ 1] == 2)
    partner = [(i, i ^ 1) for i in range(n_s)]

    def everyone(x, axis, count, **kw):
        return lax.all_to_all(
            jnp.broadcast_to(x[None], (count,) + x.shape), axis, 0, 0, **kw
        )

    sides = [
        jnp.concatenate([coupler[k], damping[k : k + 1], bounds[k : k + 1]], axis=0)
        for k in range(2)
    ]
    side_moved = lax.ppermute(sides[1], "scen", partner)
    gram1 = gram(1, n_z, matrices, ratios)
    gram_moved = lax.ppermute(gram1, "scen", partner)
    gram0 = gram(0, n_z, matrices, ratios)
    side = jnp.where(own, sides[0], side_moved)
    link = side[:rows]
    reg_row = side[rows : rows + 1].astype(F32)
    b_row = side[rows + 1 : rows + 2].astype(F32)
    share = n0 // n_z
    width = -(-(share + 1) // B) * B
    rhs = jnp.concatenate(
        [
            lax.dynamic_slice(link, (0, zpos * share), (rows, share)),
            side[rows + 1][:, None],
            jnp.zeros((rows, width - share - 1), BF16),
        ],
        axis=1,
    )
    rhs = jnp.where(live, rhs, jnp.zeros_like(rhs))

    partial = jnp.where(own, gram0, gram_moved)
    shard = jnp.sum(lax.all_to_all(partial, "col", 0, 0), axis=0)
    g, terms = solve(everyone(shard, "col", n_z), reg_row, rhs, link)

    count = n_s // 2
    same = [[2 * i + k for i in range(count)] for k in range(2)]
    terms = terms.reshape((n_s,) + terms.shape[2:])
    mine = lax.all_to_all(terms, "scen", 0, 0, axis_index_groups=[same[0] + same[1]])
    wide = everyone(jnp.sum(mine, axis=0), "col", n_z)
    half = everyone(wide, "scen", count, axis_index_groups=same)
    other = lax.ppermute(half, "scen", partner)
    first, dual = main_solve(half, other, q_diag[None], c_vec[None], g, link, b_row)

    returned = lax.ppermute(dual, "scen", partner)
    duals, primals = primal(tallies, matrices, ratios, dual, returned)
    return first[0], duals, primals


def solution(mesh):
    body = functools.partial(local, mesh.shape["scen"], mesh.shape["col"])
    return jax.shard_map(
        body,
        mesh=mesh,
        in_specs=(
            P("scen", None, "col"),
            P("scen", "col"),
            P("scen", None),
            P("scen", None, None),
            P("scen", None),
            P(),
            P(),
            P(),
        ),
        out_specs=(P(), P("scen", None), P("scen", "col")),
        check_vma=False,
    )
```

```python
import functools

import jax
import jax.numpy as jnp
from jax import lax
from jax.experimental import pallas as pl
from jax.experimental.pallas import tpu as pltpu
from jax.sharding import PartitionSpec as P

F32 = jnp.float32
BF16 = jnp.bfloat16
B = 128
TOL2 = 1e-11
MAX_STEPS = 4096
VMEM = 20 * 2**20
STAGGER_NS = 6000


def blocks_of(rows):
    n = rows // B
    return [(i, j) for i in range(n) for j in range(i + 1)]


def mm(a, b):
    return lax.dot_general(a, b, (((1,), (0,)), ((), ())), preferred_element_type=F32)


def split3(x):
    hi = x.astype(BF16)
    rest = x - hi.astype(F32)
    mid = rest.astype(BF16)
    low = (rest - mid.astype(F32)).astype(BF16)
    return hi, mid, low


def eye_mask():
    return lax.broadcasted_iota(jnp.int32, (B, B), 0) == lax.broadcasted_iota(
        jnp.int32, (B, B), 1
    )


def gram_kernel(slot, parts, w_ref, d_ref, out_ref, scaled_ref, g_ref):
    rows = w_ref.shape[0]
    tiles = [slice(i * B, (i + 1) * B) for i in range(rows // B)]
    scale = d_ref[...].astype(F32)[slot : slot + 1]
    for at in tiles:
        scaled_ref[at, :] = (w_ref[at, :].astype(F32) * scale).astype(BF16)
    for at in tiles:
        g_ref[at, :] = lax.dot_general(
            scaled_ref[at, :], w_ref[...], (((1,), (1,)), ((), ())), preferred_element_type=F32
        )
    step = B // parts
    for b, (i, j) in enumerate(blocks_of(rows)):
        blk = g_ref[tiles[i], tiles[j]]
        if i != j:
            blk = 0.5 * (blk + g_ref[tiles[j], tiles[i]].T)
        for z in range(parts):
            out_ref[z, b * step : (b + 1) * step, :] = blk[z * step : (z + 1) * step, :]


def gram(slot, parts, matrix, ratios):
    rows, cols = matrix.shape
    height = len(blocks_of(rows)) * B // parts
    return pl.pallas_call(
        functools.partial(gram_kernel, slot, parts),
        out_shape=jax.ShapeDtypeStruct((parts, height, B), F32),
        scratch_shapes=[pltpu.VMEM((rows, cols), BF16), pltpu.VMEM((rows, rows), F32)],
        compiler_params=pltpu.CompilerParams(vmem_limit_bytes=VMEM),
        name=f"gram{slot}",
    )(matrix, ratios)


def choose_kernel(tallies_ref, own_ref, moved_ref, out_ref):
    group = lax.axis_index("scen")
    held = tallies_ref[group]

    @pl.when(lax.rem(group, 2) == 1)
    def _():
        pl.delay(STAGGER_NS)

    @pl.when(held >= 1)
    def _():
        out_ref[...] = own_ref[...]

    @pl.when(held < 1)
    def _():
        out_ref[...] = moved_ref[...]


def choose(tallies, own, moved):
    return pl.pallas_call(
        choose_kernel,
        in_specs=[pl.BlockSpec(memory_space=pltpu.SMEM)]
        + [pl.BlockSpec(memory_space=pltpu.VMEM)] * 2,
        out_shape=jax.ShapeDtypeStruct(own.shape, F32),
        compiler_params=pltpu.CompilerParams(vmem_limit_bytes=VMEM),
        name="choose",
    )(tallies, own, moved)


def spread_kernel(recv_ref, out_ref):
    total = recv_ref[0]
    for z in range(1, recv_ref.shape[0]):
        total = total + recv_ref[z]
    for z in range(recv_ref.shape[0]):
        out_ref[z] = total


def spread(received):
    return pl.pallas_call(
        spread_kernel,
        out_shape=jax.ShapeDtypeStruct(received.shape, F32),
        compiler_params=pltpu.CompilerParams(vmem_limit_bytes=VMEM),
        name="spread",
    )(received)


def ratio(a, b):
    ok = b > 0.0
    return jnp.where(ok, a / jnp.where(ok, b, 1.0), 0.0)


def low_lanes(shape):
    return lax.broadcasted_iota(jnp.int32, shape, len(shape) - 1) < B // 2


def cg_block(pieces, x_ref, r_ref, p_ref, s_ref, rb_ref, sc_ref):
    hi, mid = pieces
    rows = x_ref.shape[0]
    tiles = [slice(i * B, (i + 1) * B) for i in range(rows // B)]

    def body(carry):
        k, _ = carry
        rb = rb_ref[...]
        gamma, old, was, bound = (sc_ref[i : i + 1, :] for i in range(4))
        delta = jnp.zeros_like(gamma)
        for at in tiles:
            w = mm(hi[at, :], rb) + mm(mid[at, :], rb)
            x_ref[at, :] += was * p_ref[at, :]
            p_ref[at, :] = rb_ref[at, :].astype(F32) + ratio(gamma, old) * p_ref[at, :]
            s_ref[at, :] = w + ratio(gamma, old) * s_ref[at, :]
            delta += jnp.sum(p_ref[at, :] * s_ref[at, :], axis=0, keepdims=True)
        alpha = ratio(gamma, delta)
        new = jnp.zeros_like(gamma)
        size = jnp.zeros_like(gamma)
        for at in tiles:
            r = r_ref[at, :] - alpha * s_ref[at, :]
            r_ref[at, :] = r
            rounded = r.astype(BF16)
            rb_ref[at, :] = rounded
            new += jnp.sum(r * rounded.astype(F32), axis=0, keepdims=True)
        sc_ref[0:1, :] = new
        sc_ref[1:2, :] = gamma
        sc_ref[2:3, :] = alpha
        return k + 1, jnp.max(gamma - bound)

    rhs = r_ref[...]
    x_ref[...] = jnp.zeros_like(rhs)
    p_ref[...] = jnp.zeros_like(rhs)
    s_ref[...] = jnp.zeros_like(rhs)
    rounded = rhs.astype(BF16)
    rb_ref[...] = rounded
    first = jnp.sum(rhs * rounded.astype(F32), axis=0, keepdims=True)
    sc_ref[0:1, :] = first
    sc_ref[1:3, :] = jnp.zeros((2,) + first.shape[1:], F32)
    sc_ref[3:4, :] = TOL2 * first
    lax.while_loop(
        lambda c: (c[0] < MAX_STEPS) & (c[1] > 0.0), body, (jnp.int32(0), jnp.max(first))
    )
    for at in tiles:
        x_ref[at, :] += sc_ref[2:3, :] * p_ref[at, :]


def solve_kernel(
    recv_ref, reg_ref, rhs_ref, link_ref, g_ref, out_ref,
    hi_ref, mid_ref, x_ref, r_ref, p_ref, s_ref, rb_ref, sc_ref,
):
    parts = recv_ref.shape[0]
    rows = g_ref.shape[0]
    step = B // parts
    eye = eye_mask()
    for b, (i, j) in enumerate(blocks_of(rows)):
        ri, rj = slice(i * B, (i + 1) * B), slice(j * B, (j + 1) * B)
        blk = jnp.concatenate(
            [recv_ref[z, b * step : (b + 1) * step, :] for z in range(parts)], axis=0
        )
        other = blk.T
        if i == j:
            blk = 0.5 * (blk + other) + jnp.where(eye, reg_ref[:, rj], 0.0)
        g_ref[ri, rj] = blk
        hi_ref[ri, rj], mid_ref[ri, rj] = split3(blk)[:2]
        if i != j:
            g_ref[rj, ri] = other
            hi_ref[rj, ri], mid_ref[rj, ri] = split3(other)[:2]
    r_ref[...] = rhs_ref[...].astype(F32)
    cg_block((hi_ref, mid_ref), x_ref, r_ref, p_ref, s_ref, rb_ref, sc_ref)
    n = x_ref.shape[1]
    pieces = jnp.concatenate(split3(x_ref[...]), axis=1)
    y = lax.dot_general(
        link_ref[...], pieces, (((0,), (0,)), ((), ())), preferred_element_type=F32
    )
    y = y[:, :n] + (y[:, n : 2 * n] + y[:, 2 * n :])
    half, quarter = B // 2, B // 4
    after = lax.rem(lax.axis_index("col") + 1, n0_blocks(rows))
    row = lax.broadcasted_iota(jnp.int32, y.shape, 0)
    lane = lax.broadcasted_iota(jnp.int32, y.shape, 1)
    start = after * half
    here = (row >= start) & (row < start + half) & (lane == 0)
    x_ref[...] = jnp.where(here, pltpu.roll(y, half, 1), y)
    low = low_lanes((quarter, B))
    for t in range(rows // B):
        for c in range(2):
            at = t * B + c * quarter
            up = pltpu.roll(x_ref[at + half : at + half + quarter, :], half, 1)
            out_ref[c, :, t, :] = jnp.where(low, x_ref[at : at + quarter, :], up)


def n0_blocks(rows):
    return rows // (B // 2)


def solve(received, reg_row, rhs, link):
    rows, width = rhs.shape
    return pl.pallas_call(
        solve_kernel,
        out_shape=(
            jax.ShapeDtypeStruct((rows, rows), F32),
            jax.ShapeDtypeStruct((2, B // 4, rows // B, B), F32),
        ),
        scratch_shapes=[pltpu.VMEM((rows, rows), BF16)] * 2
        + [pltpu.VMEM((rows, width), F32)] * 4
        + [pltpu.VMEM((rows, width), BF16), pltpu.VMEM((8, width), F32)],
        compiler_params=pltpu.CompilerParams(vmem_limit_bytes=VMEM),
        name="solve",
    )(received, reg_row, rhs, link)


def as_row(col, eye):
    return jnp.sum(jnp.where(eye, col, 0.0), axis=0, keepdims=True)


def as_col(row, eye):
    return jnp.sum(jnp.where(eye, row, 0.0), axis=1, keepdims=True)


def times_row(mat_ref, row, eye):
    rows = mat_ref.shape[0]
    out = []
    for i in range(rows // B):
        part = mat_ref[i * B : (i + 1) * B, :].astype(F32) * row
        out.append(as_row(jnp.sum(part, axis=1, keepdims=True), eye))
    return jnp.concatenate(out, axis=1)


def sym_times_row(mat_ref, row, eye):
    total = None
    for i in range(mat_ref.shape[0] // B):
        at = slice(i * B, (i + 1) * B)
        part = jnp.sum(mat_ref[at, :] * as_col(row[:, at], eye), axis=0, keepdims=True)
        total = part if total is None else total + part
    return total


def lane_sum(row):
    return jnp.sum(row, axis=1, keepdims=True)


def cg_row(mat_ref, rhs, x_ref, r_ref, p_ref, s_ref, sc_ref, eye):
    def body(carry):
        k, _ = carry
        old, bound, scale = (sc_ref[i : i + 1, 0:1] for i in range(3))
        r = r_ref[...]
        gamma = lane_sum(r * r)
        w = sym_times_row(mat_ref, r, eye)
        delta = lane_sum(r * w)
        beta = ratio(gamma, old)
        alpha = ratio(gamma, delta - beta * gamma * scale)
        p = r + beta * p_ref[...]
        s = w + beta * s_ref[...]
        p_ref[...] = p
        s_ref[...] = s
        x_ref[...] += alpha * p
        r_ref[...] = r - alpha * s
        sc_ref[0:1, 0:1] = gamma
        sc_ref[2:3, 0:1] = ratio(jnp.ones_like(alpha), alpha)
        return k + 1, jnp.max(gamma - bound)

    zero = jnp.zeros_like(rhs)
    x_ref[...] = zero
    p_ref[...] = zero
    s_ref[...] = zero
    r_ref[...] = rhs
    first = lane_sum(rhs * rhs)
    sc_ref[0:1, 0:1] = jnp.zeros_like(first)
    sc_ref[1:2, 0:1] = TOL2 * first
    sc_ref[2:3, 0:1] = jnp.zeros_like(first)
    lax.while_loop(
        lambda c: (c[0] < MAX_STEPS) & (c[1] > 0.0), body, (jnp.int32(0), jnp.max(first))
    )
    return x_ref[...]


def main_kernel(
    mine_ref, other_ref, q_ref, c_ref, g_ref, link_ref, b_ref, first_ref, dual_ref,
    m_ref, x_ref, r_ref, p_ref, s_ref, sc_ref,
):
    quarter, shards, tiles, _ = mine_ref.shape
    half = 2 * quarter
    eye = eye_mask()
    core = lax.rem(lax.axis_index("scen"), 2)
    low = low_lanes((quarter, B))
    for src, which in ((mine_ref, core), (other_ref, 1 - core)):
        for t in range(tiles):
            top = pl.multiple_of(which * quarter + t * B, quarter)
            for m in range(shards // 2):
                v0, v1 = src[:, 2 * m, t, :], src[:, 2 * m + 1, t, :]
                at = slice(m * B, (m + 1) * B)
                m_ref[pl.ds(top, quarter), at] = jnp.where(low, v0, pltpu.roll(v1, half, 1))
                m_ref[pl.ds(top + half, quarter), at] = jnp.where(
                    low, pltpu.roll(v0, half, 1), v1
                )
    row = lax.broadcasted_iota(jnp.int32, (B, B), 0)
    lane = lax.broadcasted_iota(jnp.int32, (B, B), 1)
    rho = []
    for t in range(tiles):
        at = slice(t * B, (t + 1) * B)
        e = (t + tiles - 1) % tiles
        before = slice(e * B, (e + 1) * B)
        near, far = m_ref[at, at], m_ref[at, before]
        rho.append(as_row(jnp.where(row[:, :1] < half, far[:, half : half + 1], near[:, :1]), eye))
        give = jnp.where(
            lane[:1] < half,
            m_ref[e * B + half : e * B + half + 1, at],
            m_ref[t * B : t * B + 1, at],
        )
        give = as_col(give, eye)
        m_ref[at, at] = jnp.where((row >= half) & (lane == 0), give, near) + jnp.where(
            eye, q_ref[:, at], 0.0
        )
        m_ref[at, before] = jnp.where((row < half) & (lane == half), give, far)
    rhs = c_ref[...] - jnp.concatenate(rho, axis=1)
    refs = (x_ref, r_ref, p_ref, s_ref, sc_ref)
    first = cg_row(m_ref, rhs, *refs, eye)
    first_ref[...] = first
    pushed = b_ref[...] + times_row(link_ref, first, eye)
    dual_ref[...] = cg_row(g_ref, pushed, *refs, eye)


def main_solve(mine, other, q_row, c_row, g, link, b_row):
    n0, rows = q_row.shape[1], b_row.shape[1]
    return pl.pallas_call(
        main_kernel,
        out_shape=(
            jax.ShapeDtypeStruct((1, n0), F32),
            jax.ShapeDtypeStruct((1, rows), F32),
        ),
        scratch_shapes=[pltpu.VMEM((n0, n0), F32)]
        + [pltpu.VMEM((1, n0), F32)] * 4
        + [pltpu.VMEM((8, B), F32)],
        compiler_params=pltpu.CompilerParams(vmem_limit_bytes=VMEM),
        name="main_solve",
    )(mine, other, q_row, c_row, g, link, b_row)


def primal_kernel(tallies_ref, w_ref, d_ref, dual_ref, back_ref, y_ref, out_ref):
    held = tallies_ref[lax.axis_index("scen")]
    scale = d_ref[...].astype(F32)
    for slot, source in enumerate((dual_ref, back_ref)):
        dual = source[...]
        dual = jnp.where(held > slot, dual, jnp.zeros_like(dual))
        y_ref[slot : slot + 1, :] = dual
        out_ref[slot : slot + 1, :] = scale[slot : slot + 1] * mm(
            dual.astype(BF16), w_ref[slot]
        )


def primal(tallies, matrices, ratios, dual, back):
    return pl.pallas_call(
        primal_kernel,
        in_specs=[pl.BlockSpec(memory_space=pltpu.SMEM)]
        + [pl.BlockSpec(memory_space=pltpu.VMEM)] * 4,
        out_shape=(
            jax.ShapeDtypeStruct((2, dual.shape[1]), F32),
            jax.ShapeDtypeStruct(ratios.shape, F32),
        ),
        compiler_params=pltpu.CompilerParams(vmem_limit_bytes=VMEM),
        name="primal",
    )(tallies, matrices, ratios, dual, back)


def local(
    scen_size, col_size, matrices, ratios, damping, coupler, bounds, q_diag, c_vec, tallies
):
    n_s, n_z = scen_size, col_size
    rows = matrices.shape[1]
    n0 = coupler.shape[2]
    pos = lax.axis_index("scen")
    zpos = lax.axis_index("col")
    held = tallies[pos]
    own = held >= 1
    live = own | (tallies[pos ^ 1] == 2)
    partner = [(i, i ^ 1) for i in range(n_s)]

    def everyone(x, axis, count, **kw):
        return lax.all_to_all(
            jnp.broadcast_to(x[None], (count,) + x.shape), axis, 0, 0, **kw
        )

    sides = [
        jnp.concatenate([coupler[k], damping[k : k + 1], bounds[k : k + 1]], axis=0)
        for k in range(2)
    ]
    side_moved = lax.ppermute(sides[1], "scen", partner)
    gram1 = gram(1, n_z, matrices[1], ratios)
    later, gram1 = lax.optimization_barrier((matrices, gram1))
    gram_moved = lax.ppermute(gram1, "scen", partner)
    gram0 = gram(0, n_z, later[0], ratios)
    side = jnp.where(own, sides[0], side_moved)
    link = side[:rows]
    reg_row = side[rows : rows + 1].astype(F32)
    b_row = side[rows + 1 : rows + 2].astype(F32)
    share = n0 // n_z
    width = -(-(share + 1) // B) * B
    rhs = jnp.concatenate(
        [
            lax.dynamic_slice(link, (0, zpos * share), (rows, share)),
            side[rows + 1][:, None],
            jnp.zeros((rows, width - share - 1), BF16),
        ],
        axis=1,
    )
    rhs = jnp.where(live, rhs, jnp.zeros_like(rhs))

    partial = choose(tallies, gram0, gram_moved)
    shards = spread(lax.all_to_all(partial, "col", 0, 0))
    g, terms = solve(lax.all_to_all(shards, "col", 0, 0), reg_row, rhs, link)

    count = n_s // 2
    same = [[2 * i + k for i in range(count)] for k in range(2)]
    terms = terms.reshape((n_s,) + terms.shape[2:])
    mine = lax.all_to_all(terms, "scen", 0, 0, axis_index_groups=[same[0] + same[1]])
    wide = everyone(jnp.sum(mine, axis=0), "col", n_z)
    half = everyone(wide, "scen", count, axis_index_groups=same)
    other = lax.ppermute(half, "scen", partner)
    first, dual = main_solve(half, other, q_diag[None], c_vec[None], g, link, b_row)

    returned = lax.ppermute(dual, "scen", partner)
    duals, primals = primal(tallies, matrices, ratios, dual, returned)
    return first[0], duals, primals


def solution(mesh):
    body = functools.partial(local, mesh.shape["scen"], mesh.shape["col"])
    return jax.shard_map(
        body,
        mesh=mesh,
        in_specs=(
            P("scen", None, "col"),
            P("scen", "col"),
            P("scen", None),
            P("scen", None, None),
            P("scen", None),
            P(),
            P(),
            P(),
        ),
        out_specs=(P(), P("scen", None), P("scen", "col")),
        check_vma=False,
    )
```

```python
import functools

import jax
import jax.numpy as jnp
from jax import lax
from jax.experimental import pallas as pl
from jax.experimental.pallas import tpu as pltpu
from jax.sharding import PartitionSpec as P

F32 = jnp.float32
BF16 = jnp.bfloat16
F16 = jnp.float16
B = 128
TOL2 = 1e-11
MAX_STEPS = 4096
VMEM = 20 * 2**20
WIDE_VMEM = 50 * 2**20
SLABS = 16
STAGGER_NS = 4000


def blocks_of(rows):
    n = rows // B
    return [(i, j) for i in range(n) for j in range(i + 1)]


def mm(a, b):
    return lax.dot_general(a, b, (((1,), (0,)), ((), ())), preferred_element_type=F32)


def split3(x):
    hi = x.astype(BF16)
    rest = x - hi.astype(F32)
    mid = rest.astype(BF16)
    low = (rest - mid.astype(F32)).astype(BF16)
    return hi, mid, low


def eye_mask():
    return lax.broadcasted_iota(jnp.int32, (B, B), 0) == lax.broadcasted_iota(
        jnp.int32, (B, B), 1
    )


def gram_kernel(slot, parts, w_ref, d_ref, out_ref, scaled_ref, g_ref):
    if slot == 0:
        @pl.when(lax.rem(lax.axis_index("scen"), 2) == 1)
        def _():
            pl.delay(STAGGER_NS)

    rows = w_ref.shape[0]
    tiles = [slice(i * B, (i + 1) * B) for i in range(rows // B)]
    scale = d_ref[...].astype(F32)[slot : slot + 1]
    for at in tiles:
        scaled_ref[at, :] = (w_ref[at, :].astype(F32) * scale).astype(BF16)
    for at in tiles:
        g_ref[at, :] = lax.dot_general(
            scaled_ref[at, :], w_ref[...], (((1,), (1,)), ((), ())), preferred_element_type=F32
        )
    step = B // parts
    for b, (i, j) in enumerate(blocks_of(rows)):
        blk = g_ref[tiles[i], tiles[j]]
        if i != j:
            blk = 0.5 * (blk + g_ref[tiles[j], tiles[i]].T)
        for z in range(parts):
            out_ref[z, b * step : (b + 1) * step, :] = blk[z * step : (z + 1) * step, :]


def gram(slot, parts, matrix, ratios):
    rows, cols = matrix.shape
    height = len(blocks_of(rows)) * B // parts
    return pl.pallas_call(
        functools.partial(gram_kernel, slot, parts),
        out_shape=jax.ShapeDtypeStruct((parts, height, B), F32),
        scratch_shapes=[pltpu.VMEM((rows, cols), BF16), pltpu.VMEM((rows, rows), F32)],
        compiler_params=pltpu.CompilerParams(vmem_limit_bytes=VMEM),
        name=f"gram{slot}",
    )(matrix, ratios)


def ratio(a, b):
    ok = b > 0.0
    return jnp.where(ok, a / jnp.where(ok, b, 1.0), 0.0)


def low_lanes(shape):
    return lax.broadcasted_iota(jnp.int32, shape, len(shape) - 1) < B // 2


def cg_block(pieces, x_ref, r_ref, p_ref, s_ref, rb_ref, sc_ref):
    hi, mid = pieces
    rows = x_ref.shape[0]
    tiles = [slice(i * B, (i + 1) * B) for i in range(rows // B)]

    def body(carry):
        k, _ = carry
        rb = rb_ref[...]
        gamma, old, was, bound = (sc_ref[i : i + 1, :] for i in range(4))
        delta = jnp.zeros_like(gamma)
        for at in tiles:
            w = mm(hi[at, :], rb) + mm(mid[at, :], rb)
            x_ref[at, :] += was * p_ref[at, :]
            p_ref[at, :] = rb_ref[at, :].astype(F32) + ratio(gamma, old) * p_ref[at, :]
            s_ref[at, :] = w + ratio(gamma, old) * s_ref[at, :]
            delta += jnp.sum(p_ref[at, :] * s_ref[at, :], axis=0, keepdims=True)
        alpha = ratio(gamma, delta)
        new = jnp.zeros_like(gamma)
        size = jnp.zeros_like(gamma)
        for at in tiles:
            r = r_ref[at, :] - alpha * s_ref[at, :]
            r_ref[at, :] = r
            rounded = r.astype(BF16)
            rb_ref[at, :] = rounded
            new += jnp.sum(r * rounded.astype(F32), axis=0, keepdims=True)
        sc_ref[0:1, :] = new
        sc_ref[1:2, :] = gamma
        sc_ref[2:3, :] = alpha
        return k + 1, jnp.max(gamma - bound)

    rhs = r_ref[...]
    x_ref[...] = jnp.zeros_like(rhs)
    p_ref[...] = jnp.zeros_like(rhs)
    s_ref[...] = jnp.zeros_like(rhs)
    rounded = rhs.astype(BF16)
    rb_ref[...] = rounded
    first = jnp.sum(rhs * rounded.astype(F32), axis=0, keepdims=True)
    sc_ref[0:1, :] = first
    sc_ref[1:3, :] = jnp.zeros((2,) + first.shape[1:], F32)
    sc_ref[3:4, :] = TOL2 * first
    lax.while_loop(
        lambda c: (c[0] < MAX_STEPS) & (c[1] > 0.0), body, (jnp.int32(0), jnp.max(first))
    )
    for at in tiles:
        x_ref[at, :] += sc_ref[2:3, :] * p_ref[at, :]


def solve_kernel(
    recv_ref, reg_ref, rhs_ref, link_ref, g_hbm, out_ref,
    g_ref, hi_ref, mid_ref, x_ref, r_ref, p_ref, s_ref, rb_ref, sc_ref, sem,
):
    parts = recv_ref.shape[0]
    rows = g_ref.shape[0]
    step = B // parts
    eye = eye_mask()
    for b, (i, j) in enumerate(blocks_of(rows)):
        ri, rj = slice(i * B, (i + 1) * B), slice(j * B, (j + 1) * B)
        blk = jnp.concatenate(
            [recv_ref[z, b * step : (b + 1) * step, :] for z in range(parts)], axis=0
        )
        other = blk.T
        if i == j:
            blk = 0.5 * (blk + other) + jnp.where(eye, reg_ref[:, rj], 0.0)
        g_ref[ri, rj] = blk
        hi_ref[ri, rj], mid_ref[ri, rj] = split3(blk)[:2]
        if i != j:
            g_ref[rj, ri] = other
            hi_ref[rj, ri], mid_ref[rj, ri] = split3(other)[:2]
    keep = pltpu.make_async_copy(g_ref, g_hbm.at[0], sem)
    keep.start()
    r_ref[...] = rhs_ref[...].astype(F32)
    cg_block((hi_ref, mid_ref), x_ref, r_ref, p_ref, s_ref, rb_ref, sc_ref)
    n = x_ref.shape[1]
    pieces = jnp.concatenate(split3(x_ref[...]), axis=1)
    y = lax.dot_general(
        link_ref[...], pieces, (((0,), (0,)), ((), ())), preferred_element_type=F32
    )
    y = y[:, :n] + (y[:, n : 2 * n] + y[:, 2 * n :])
    half, quarter = B // 2, B // 4
    after = lax.rem(lax.axis_index("col") + 1, n0_blocks(rows))
    row = lax.broadcasted_iota(jnp.int32, y.shape, 0)
    lane = lax.broadcasted_iota(jnp.int32, y.shape, 1)
    start = after * half
    here = (row >= start) & (row < start + half) & (lane == 0)
    x_ref[...] = jnp.where(here, pltpu.roll(y, half, 1), y)
    low = low_lanes((quarter, B))
    for t in range(rows // B):
        for c in range(2):
            at = t * B + c * quarter
            up = pltpu.roll(x_ref[at + half : at + half + quarter, :], half, 1)
            out_ref[c, :, t, :] = jnp.where(low, x_ref[at : at + quarter, :], up)
    keep.wait()


def n0_blocks(rows):
    return rows // (B // 2)


def solve(received, reg_row, rhs, link):
    rows, width = rhs.shape
    return pl.pallas_call(
        solve_kernel,
        out_shape=(
            jax.ShapeDtypeStruct((SLABS, rows, rows), F32),
            jax.ShapeDtypeStruct((2, B // 4, rows // B, B), F32),
        ),
        in_specs=[pl.BlockSpec(memory_space=pltpu.VMEM)] * 4,
        out_specs=(
            pl.BlockSpec(memory_space=pl.ANY),
            pl.BlockSpec(memory_space=pltpu.VMEM),
        ),
        scratch_shapes=[pltpu.VMEM((rows, rows), F32)]
        + [pltpu.VMEM((rows, rows), BF16)] * 2
        + [pltpu.VMEM((rows, width), F32)] * 4
        + [pltpu.VMEM((rows, width), BF16), pltpu.VMEM((8, width), F32)]
        + [pltpu.SemaphoreType.DMA],
        compiler_params=pltpu.CompilerParams(vmem_limit_bytes=WIDE_VMEM),
        name="solve",
    )(received, reg_row, rhs, link)


def as_row(col, eye):
    return jnp.sum(jnp.where(eye, col, 0.0), axis=0, keepdims=True)


def as_col(row, eye):
    return jnp.sum(jnp.where(eye, row, 0.0), axis=1, keepdims=True)


def times_row(mat_ref, row, eye):
    rows = mat_ref.shape[0]
    out = []
    for i in range(rows // B):
        part = mat_ref[i * B : (i + 1) * B, :].astype(F32) * row
        out.append(as_row(jnp.sum(part, axis=1, keepdims=True), eye))
    return jnp.concatenate(out, axis=1)


def sym_times_row(mat_ref, row, eye):
    total = None
    for i in range(mat_ref.shape[0] // B):
        at = slice(i * B, (i + 1) * B)
        part = jnp.sum(mat_ref[at, :] * as_col(row[:, at], eye), axis=0, keepdims=True)
        total = part if total is None else total + part
    return total


def lane_sum(row):
    return jnp.sum(row, axis=1, keepdims=True)


def cg_row(mat_ref, rhs, x_ref, r_ref, p_ref, s_ref, sc_ref, eye):
    def body(carry):
        k, _ = carry
        old, bound, scale = (sc_ref[i : i + 1, 0:1] for i in range(3))
        r = r_ref[...]
        gamma = lane_sum(r * r)
        w = sym_times_row(mat_ref, r, eye)
        delta = lane_sum(r * w)
        beta = ratio(gamma, old)
        alpha = ratio(gamma, delta - beta * gamma * scale)
        p = r + beta * p_ref[...]
        s = w + beta * s_ref[...]
        p_ref[...] = p
        s_ref[...] = s
        x_ref[...] += alpha * p
        r_ref[...] = r - alpha * s
        sc_ref[0:1, 0:1] = gamma
        sc_ref[2:3, 0:1] = ratio(jnp.ones_like(alpha), alpha)
        return k + 1, jnp.max(gamma - bound)

    zero = jnp.zeros_like(rhs)
    x_ref[...] = zero
    p_ref[...] = zero
    s_ref[...] = zero
    r_ref[...] = rhs
    first = lane_sum(rhs * rhs)
    sc_ref[0:1, 0:1] = jnp.zeros_like(first)
    sc_ref[1:2, 0:1] = TOL2 * first
    sc_ref[2:3, 0:1] = jnp.zeros_like(first)
    lax.while_loop(
        lambda c: (c[0] < MAX_STEPS) & (c[1] > 0.0), body, (jnp.int32(0), jnp.max(first))
    )
    return x_ref[...]


def main_kernel(
    mine_ref, other_ref, q_ref, c_ref, g_hbm, link_ref, b_ref, first_ref, dual_ref,
    m_ref, g_ref, x_ref, r_ref, p_ref, s_ref, sc_ref, sem,
):
    load = pltpu.make_async_copy(g_hbm.at[0], g_ref, sem)
    load.start()
    quarter, shards, tiles, _ = mine_ref.shape
    half = 2 * quarter
    eye = eye_mask()
    core = lax.rem(lax.axis_index("scen"), 2)
    low = low_lanes((quarter, B))
    for src, which in ((mine_ref, core), (other_ref, 1 - core)):
        for t in range(tiles):
            top = pl.multiple_of(which * quarter + t * B, quarter)
            for m in range(shards // 2):
                v0, v1 = src[:, 2 * m, t, :], src[:, 2 * m + 1, t, :]
                at = slice(m * B, (m + 1) * B)
                m_ref[pl.ds(top, quarter), at] = jnp.where(low, v0, pltpu.roll(v1, half, 1))
                m_ref[pl.ds(top + half, quarter), at] = jnp.where(
                    low, pltpu.roll(v0, half, 1), v1
                )
    row = lax.broadcasted_iota(jnp.int32, (B, B), 0)
    lane = lax.broadcasted_iota(jnp.int32, (B, B), 1)
    rho = []
    for t in range(tiles):
        at = slice(t * B, (t + 1) * B)
        e = (t + tiles - 1) % tiles
        before = slice(e * B, (e + 1) * B)
        near, far = m_ref[at, at], m_ref[at, before]
        rho.append(as_row(jnp.where(row[:, :1] < half, far[:, half : half + 1], near[:, :1]), eye))
        give = jnp.where(
            lane[:1] < half,
            m_ref[e * B + half : e * B + half + 1, at],
            m_ref[t * B : t * B + 1, at],
        )
        give = as_col(give, eye)
        m_ref[at, at] = jnp.where((row >= half) & (lane == 0), give, near) + jnp.where(
            eye, q_ref[:, at], 0.0
        )
        m_ref[at, before] = jnp.where((row < half) & (lane == half), give, far)
    rhs = c_ref[...] - jnp.concatenate(rho, axis=1)
    refs = (x_ref, r_ref, p_ref, s_ref, sc_ref)
    first = cg_row(m_ref, rhs, *refs, eye)
    first_ref[...] = first
    pushed = b_ref[...] + times_row(link_ref, first, eye)
    load.wait()
    dual_ref[...] = cg_row(g_ref, pushed, *refs, eye)


def main_solve(mine, other, q_row, c_row, g, link, b_row):
    n0, rows = q_row.shape[1], b_row.shape[1]
    return pl.pallas_call(
        main_kernel,
        out_shape=(
            jax.ShapeDtypeStruct((1, n0), F32),
            jax.ShapeDtypeStruct((1, rows), F32),
        ),
        in_specs=[pl.BlockSpec(memory_space=pltpu.VMEM)] * 4
        + [pl.BlockSpec(memory_space=pl.ANY)]
        + [pl.BlockSpec(memory_space=pltpu.VMEM)] * 2,
        scratch_shapes=[pltpu.VMEM((n0, n0), F32), pltpu.VMEM((rows, rows), F32)]
        + [pltpu.VMEM((1, n0), F32)] * 4
        + [pltpu.VMEM((8, B), F32), pltpu.SemaphoreType.DMA],
        compiler_params=pltpu.CompilerParams(vmem_limit_bytes=WIDE_VMEM),
        name="main_solve",
    )(mine, other, q_row, c_row, g, link, b_row)


def primal_kernel(tallies_ref, w_ref, d_ref, dual_ref, back_ref, y_ref, out_ref):
    held = tallies_ref[lax.axis_index("scen")]
    scale = d_ref[...].astype(F32)
    for slot, source in enumerate((dual_ref, back_ref)):
        dual = source[...]
        dual = jnp.where(held > slot, dual, jnp.zeros_like(dual))
        y_ref[slot : slot + 1, :] = dual
        out_ref[slot : slot + 1, :] = scale[slot : slot + 1] * mm(
            dual.astype(BF16), w_ref[slot]
        )


def primal(tallies, matrices, ratios, dual, back):
    return pl.pallas_call(
        primal_kernel,
        in_specs=[pl.BlockSpec(memory_space=pltpu.SMEM)]
        + [pl.BlockSpec(memory_space=pltpu.VMEM)] * 4,
        out_shape=(
            jax.ShapeDtypeStruct((2, dual.shape[1]), F32),
            jax.ShapeDtypeStruct(ratios.shape, F32),
        ),
        compiler_params=pltpu.CompilerParams(vmem_limit_bytes=VMEM),
        name="primal",
    )(tallies, matrices, ratios, dual, back)


def local(
    scen_size, col_size, matrices, ratios, damping, coupler, bounds, q_diag, c_vec, tallies
):
    n_s, n_z = scen_size, col_size
    rows = matrices.shape[1]
    n0 = coupler.shape[2]
    pos = lax.axis_index("scen")
    zpos = lax.axis_index("col")
    held = tallies[pos]
    own = held >= 1
    live = own | (tallies[pos ^ 1] == 2)
    partner = [(i, i ^ 1) for i in range(n_s)]

    def everyone(x, axis, count, **kw):
        return lax.all_to_all(
            jnp.broadcast_to(x[None], (count,) + x.shape), axis, 0, 0, **kw
        )

    sides = [
        jnp.concatenate([coupler[k], damping[k : k + 1], bounds[k : k + 1]], axis=0)
        for k in range(2)
    ]
    side_moved = lax.ppermute(sides[1], "scen", partner)
    gram1 = gram(1, n_z, matrices[1], ratios)
    later, gram1 = lax.optimization_barrier((matrices, gram1))
    gram_moved = lax.ppermute(gram1, "scen", partner)
    gram0 = gram(0, n_z, later[0], ratios)
    side = jnp.where(own, sides[0], side_moved)
    link = side[:rows]
    reg_row = side[rows : rows + 1].astype(F32)
    b_row = side[rows + 1 : rows + 2].astype(F32)
    share = n0 // n_z
    width = -(-(share + 1) // B) * B
    rhs = jnp.concatenate(
        [
            lax.dynamic_slice(link, (0, zpos * share), (rows, share)),
            side[rows + 1][:, None],
            jnp.zeros((rows, width - share - 1), BF16),
        ],
        axis=1,
    )
    rhs = jnp.where(live, rhs, jnp.zeros_like(rhs))

    partial = jnp.where(own, gram0, gram_moved).astype(F16)
    received = lax.all_to_all(partial, "col", 0, 0).astype(F32)
    whole = everyone(jnp.sum(received, axis=0).astype(F16), "col", n_z)
    g, terms = solve(whole.astype(F32), reg_row, rhs, link)

    count = n_s // 2
    same = [[2 * i + k for i in range(count)] for k in range(2)]
    terms = terms.reshape((n_s,) + terms.shape[2:])
    mine = lax.all_to_all(terms, "scen", 0, 0, axis_index_groups=[same[0] + same[1]])
    wide = everyone(jnp.sum(mine, axis=0), "col", n_z)
    half = everyone(wide, "scen", count, axis_index_groups=same)
    other = lax.ppermute(half, "scen", partner)
    first, dual = main_solve(half, other, q_diag[None], c_vec[None], g, link, b_row)

    returned = lax.ppermute(dual, "scen", partner)
    duals, primals = primal(tallies, matrices, ratios, dual, returned)
    return first[0], duals, primals


def solution(mesh):
    body = functools.partial(local, mesh.shape["scen"], mesh.shape["col"])
    return jax.shard_map(
        body,
        mesh=mesh,
        in_specs=(
            P("scen", None, "col"),
            P("scen", "col"),
            P("scen", None),
            P("scen", None, None),
            P("scen", None),
            P(),
            P(),
            P(),
        ),
        out_specs=(P(), P("scen", None), P("scen", "col")),
        check_vma=False,
    )
```

```python
import functools

import jax
import jax.numpy as jnp
from jax import lax
from jax.experimental import pallas as pl
from jax.experimental.pallas import tpu as pltpu
from jax.sharding import PartitionSpec as P

F32 = jnp.float32
BF16 = jnp.bfloat16
F16 = jnp.float16
B = 128
TOL2 = 1e-11
MAX_STEPS = 4096
VMEM = 20 * 2**20
WIDE_VMEM = 50 * 2**20
SLABS = 16
RHO_SCALE = 0.25
STAGGER_NS = 2500


def blocks_of(rows):
    n = rows // B
    return [(i, j) for i in range(n) for j in range(i + 1)]


def mm(a, b):
    return lax.dot_general(a, b, (((1,), (0,)), ((), ())), preferred_element_type=F32)


def split3(x):
    hi = x.astype(BF16)
    rest = x - hi.astype(F32)
    mid = rest.astype(BF16)
    low = (rest - mid.astype(F32)).astype(BF16)
    return hi, mid, low


def eye_mask():
    return lax.broadcasted_iota(jnp.int32, (B, B), 0) == lax.broadcasted_iota(
        jnp.int32, (B, B), 1
    )


def gram_kernel(slot, parts, w_ref, d_ref, out_ref, scaled_ref, g_ref):
    if slot == 0:
        @pl.when(lax.rem(lax.axis_index("scen"), 2) == 1)
        def _():
            pl.delay(STAGGER_NS)

    rows = w_ref.shape[0]
    tiles = [slice(i * B, (i + 1) * B) for i in range(rows // B)]
    scale = d_ref[...].astype(F32)[slot : slot + 1]
    for at in tiles:
        scaled_ref[at, :] = (w_ref[at, :].astype(F32) * scale).astype(BF16)
    for at in tiles:
        g_ref[at, :] = lax.dot_general(
            scaled_ref[at, :], w_ref[...], (((1,), (1,)), ((), ())), preferred_element_type=F32
        )
    step = B // parts
    for b, (i, j) in enumerate(blocks_of(rows)):
        blk = g_ref[tiles[i], tiles[j]]
        if i != j:
            blk = 0.5 * (blk + g_ref[tiles[j], tiles[i]].T)
        for z in range(parts):
            out_ref[z, b * step : (b + 1) * step, :] = blk[z * step : (z + 1) * step, :]


def gram(slot, parts, matrix, ratios):
    rows, cols = matrix.shape
    height = len(blocks_of(rows)) * B // parts
    return pl.pallas_call(
        functools.partial(gram_kernel, slot, parts),
        out_shape=jax.ShapeDtypeStruct((parts, height, B), F32),
        scratch_shapes=[pltpu.VMEM((rows, cols), BF16), pltpu.VMEM((rows, rows), F32)],
        compiler_params=pltpu.CompilerParams(vmem_limit_bytes=VMEM),
        name=f"gram{slot}",
    )(matrix, ratios)


def ratio(a, b):
    ok = b > 0.0
    return jnp.where(ok, a / jnp.where(ok, b, 1.0), 0.0)


def low_lanes(shape):
    return lax.broadcasted_iota(jnp.int32, shape, len(shape) - 1) < B // 2


def cg_block(pieces, x_ref, r_ref, p_ref, s_ref, rb_ref, sc_ref):
    hi, mid = pieces
    rows = x_ref.shape[0]
    tiles = [slice(i * B, (i + 1) * B) for i in range(rows // B)]

    def body(carry):
        k, _ = carry
        rb = rb_ref[...]
        gamma, old, was, bound = (sc_ref[i : i + 1, :] for i in range(4))
        delta = jnp.zeros_like(gamma)
        for at in tiles:
            w = mm(hi[at, :], rb) + mm(mid[at, :], rb)
            x_ref[at, :] += was * p_ref[at, :]
            p_ref[at, :] = rb_ref[at, :].astype(F32) + ratio(gamma, old) * p_ref[at, :]
            s_ref[at, :] = w + ratio(gamma, old) * s_ref[at, :]
            delta += jnp.sum(p_ref[at, :] * s_ref[at, :], axis=0, keepdims=True)
        alpha = ratio(gamma, delta)
        new = jnp.zeros_like(gamma)
        size = jnp.zeros_like(gamma)
        for at in tiles:
            r = r_ref[at, :] - alpha * s_ref[at, :]
            r_ref[at, :] = r
            rounded = r.astype(BF16)
            rb_ref[at, :] = rounded
            new += jnp.sum(r * rounded.astype(F32), axis=0, keepdims=True)
        sc_ref[0:1, :] = new
        sc_ref[1:2, :] = gamma
        sc_ref[2:3, :] = alpha
        return k + 1, jnp.max(gamma - bound)

    rhs = r_ref[...]
    x_ref[...] = jnp.zeros_like(rhs)
    p_ref[...] = jnp.zeros_like(rhs)
    s_ref[...] = jnp.zeros_like(rhs)
    rounded = rhs.astype(BF16)
    rb_ref[...] = rounded
    first = jnp.sum(rhs * rounded.astype(F32), axis=0, keepdims=True)
    sc_ref[0:1, :] = first
    sc_ref[1:3, :] = jnp.zeros((2,) + first.shape[1:], F32)
    sc_ref[3:4, :] = TOL2 * first
    lax.while_loop(
        lambda c: (c[0] < MAX_STEPS) & (c[1] > 0.0), body, (jnp.int32(0), jnp.max(first))
    )
    for at in tiles:
        x_ref[at, :] += sc_ref[2:3, :] * p_ref[at, :]


def solve_kernel(
    recv_ref, reg_ref, rhs_ref, link_ref, g_hbm, out_ref,
    g_ref, hi_ref, mid_ref, x_ref, r_ref, p_ref, s_ref, rb_ref, sc_ref, sem,
):
    parts = recv_ref.shape[0]
    rows = g_ref.shape[0]
    step = B // parts
    eye = eye_mask()
    for b, (i, j) in enumerate(blocks_of(rows)):
        ri, rj = slice(i * B, (i + 1) * B), slice(j * B, (j + 1) * B)
        blk = jnp.concatenate(
            [recv_ref[z, b * step : (b + 1) * step, :] for z in range(parts)], axis=0
        )
        other = blk.T
        if i == j:
            blk = 0.5 * (blk + other) + jnp.where(eye, reg_ref[:, rj], 0.0)
        g_ref[ri, rj] = blk
        hi_ref[ri, rj], mid_ref[ri, rj] = split3(blk)[:2]
        if i != j:
            g_ref[rj, ri] = other
            hi_ref[rj, ri], mid_ref[rj, ri] = split3(other)[:2]
    keep = pltpu.make_async_copy(g_ref, g_hbm.at[0], sem)
    keep.start()
    r_ref[...] = rhs_ref[...].astype(F32)
    cg_block((hi_ref, mid_ref), x_ref, r_ref, p_ref, s_ref, rb_ref, sc_ref)
    n = x_ref.shape[1]
    pieces = jnp.concatenate(split3(x_ref[...]), axis=1)
    y = lax.dot_general(
        link_ref[...], pieces, (((0,), (0,)), ((), ())), preferred_element_type=F32
    )
    y = y[:, :n] + (y[:, n : 2 * n] + y[:, 2 * n :])
    half, quarter = B // 2, B // 4
    after = lax.rem(lax.axis_index("col") + 1, n0_blocks(rows))
    row = lax.broadcasted_iota(jnp.int32, y.shape, 0)
    lane = lax.broadcasted_iota(jnp.int32, y.shape, 1)
    start = after * half
    here = (row >= start) & (row < start + half) & (lane == 0)
    x_ref[...] = jnp.where(here, pltpu.roll(y, half, 1) * RHO_SCALE, y)
    low = low_lanes((quarter, B))
    for t in range(rows // B):
        for c in range(2):
            at = t * B + c * quarter
            up = pltpu.roll(x_ref[at + half : at + half + quarter, :], half, 1)
            out_ref[c, :, t, :] = jnp.where(low, x_ref[at : at + quarter, :], up)
    keep.wait()


def n0_blocks(rows):
    return rows // (B // 2)


def solve(received, reg_row, rhs, link):
    rows, width = rhs.shape
    return pl.pallas_call(
        solve_kernel,
        out_shape=(
            jax.ShapeDtypeStruct((SLABS, rows, rows), F32),
            jax.ShapeDtypeStruct((2, B // 4, rows // B, B), F32),
        ),
        in_specs=[pl.BlockSpec(memory_space=pltpu.VMEM)] * 4,
        out_specs=(
            pl.BlockSpec(memory_space=pl.ANY),
            pl.BlockSpec(memory_space=pltpu.VMEM),
        ),
        scratch_shapes=[pltpu.VMEM((rows, rows), F32)]
        + [pltpu.VMEM((rows, rows), BF16)] * 2
        + [pltpu.VMEM((rows, width), F32)] * 4
        + [pltpu.VMEM((rows, width), BF16), pltpu.VMEM((8, width), F32)]
        + [pltpu.SemaphoreType.DMA],
        compiler_params=pltpu.CompilerParams(vmem_limit_bytes=WIDE_VMEM),
        name="solve",
    )(received, reg_row, rhs, link)


def as_row(col, eye):
    return jnp.sum(jnp.where(eye, col, 0.0), axis=0, keepdims=True)


def as_col(row, eye):
    return jnp.sum(jnp.where(eye, row, 0.0), axis=1, keepdims=True)


def times_row(mat_ref, row, eye):
    rows = mat_ref.shape[0]
    out = []
    for i in range(rows // B):
        part = mat_ref[i * B : (i + 1) * B, :].astype(F32) * row
        out.append(as_row(jnp.sum(part, axis=1, keepdims=True), eye))
    return jnp.concatenate(out, axis=1)


def sym_times_row(mat_ref, row, eye):
    total = None
    for i in range(mat_ref.shape[0] // B):
        at = slice(i * B, (i + 1) * B)
        part = jnp.sum(mat_ref[at, :] * as_col(row[:, at], eye), axis=0, keepdims=True)
        total = part if total is None else total + part
    return total


def lane_sum(row):
    return jnp.sum(row, axis=1, keepdims=True)


def cg_row(mat_ref, rhs, x_ref, r_ref, p_ref, s_ref, sc_ref, eye):
    def body(carry):
        k, _ = carry
        old, bound, scale = (sc_ref[i : i + 1, 0:1] for i in range(3))
        r = r_ref[...]
        gamma = lane_sum(r * r)
        w = sym_times_row(mat_ref, r, eye)
        delta = lane_sum(r * w)
        beta = ratio(gamma, old)
        alpha = ratio(gamma, delta - beta * gamma * scale)
        p = r + beta * p_ref[...]
        s = w + beta * s_ref[...]
        p_ref[...] = p
        s_ref[...] = s
        x_ref[...] += alpha * p
        r_ref[...] = r - alpha * s
        sc_ref[0:1, 0:1] = gamma
        sc_ref[2:3, 0:1] = ratio(jnp.ones_like(alpha), alpha)
        return k + 1, jnp.max(gamma - bound)

    zero = jnp.zeros_like(rhs)
    x_ref[...] = zero
    p_ref[...] = zero
    s_ref[...] = zero
    r_ref[...] = rhs
    first = lane_sum(rhs * rhs)
    sc_ref[0:1, 0:1] = jnp.zeros_like(first)
    sc_ref[1:2, 0:1] = TOL2 * first
    sc_ref[2:3, 0:1] = jnp.zeros_like(first)
    lax.while_loop(
        lambda c: (c[0] < MAX_STEPS) & (c[1] > 0.0), body, (jnp.int32(0), jnp.max(first))
    )
    return x_ref[...]


def main_kernel(
    mine_ref, other_ref, q_ref, c_ref, g_hbm, link_ref, b_ref, first_ref, dual_ref,
    m_ref, g_ref, x_ref, r_ref, p_ref, s_ref, sc_ref, sem,
):
    load = pltpu.make_async_copy(g_hbm.at[0], g_ref, sem)
    load.start()
    quarter, shards, tiles, _ = mine_ref.shape
    half = 2 * quarter
    eye = eye_mask()
    core = lax.rem(lax.axis_index("scen"), 2)
    low = low_lanes((quarter, B))
    for src, which in ((mine_ref, core), (other_ref, 1 - core)):
        for t in range(tiles):
            top = pl.multiple_of(which * quarter + t * B, quarter)
            for m in range(shards // 2):
                v0, v1 = src[:, 2 * m, t, :], src[:, 2 * m + 1, t, :]
                at = slice(m * B, (m + 1) * B)
                m_ref[pl.ds(top, quarter), at] = jnp.where(low, v0, pltpu.roll(v1, half, 1))
                m_ref[pl.ds(top + half, quarter), at] = jnp.where(
                    low, pltpu.roll(v0, half, 1), v1
                )
    row = lax.broadcasted_iota(jnp.int32, (B, B), 0)
    lane = lax.broadcasted_iota(jnp.int32, (B, B), 1)
    rho = []
    for t in range(tiles):
        at = slice(t * B, (t + 1) * B)
        e = (t + tiles - 1) % tiles
        before = slice(e * B, (e + 1) * B)
        near, far = m_ref[at, at], m_ref[at, before]
        rho.append(as_row(jnp.where(row[:, :1] < half, far[:, half : half + 1], near[:, :1]), eye))
        give = jnp.where(
            lane[:1] < half,
            m_ref[e * B + half : e * B + half + 1, at],
            m_ref[t * B : t * B + 1, at],
        )
        give = as_col(give, eye)
        m_ref[at, at] = jnp.where((row >= half) & (lane == 0), give, near) + jnp.where(
            eye, q_ref[:, at], 0.0
        )
        m_ref[at, before] = jnp.where((row < half) & (lane == half), give, far)
    rhs = c_ref[...] - jnp.concatenate(rho, axis=1) * (1.0 / RHO_SCALE)
    refs = (x_ref, r_ref, p_ref, s_ref, sc_ref)
    first = cg_row(m_ref, rhs, *refs, eye)
    first_ref[...] = first
    pushed = b_ref[...] + times_row(link_ref, first, eye)
    load.wait()
    dual_ref[...] = cg_row(g_ref, pushed, *refs, eye)


def main_solve(mine, other, q_row, c_row, g, link, b_row):
    n0, rows = q_row.shape[1], b_row.shape[1]
    return pl.pallas_call(
        main_kernel,
        out_shape=(
            jax.ShapeDtypeStruct((1, n0), F32),
            jax.ShapeDtypeStruct((1, rows), F32),
        ),
        in_specs=[pl.BlockSpec(memory_space=pltpu.VMEM)] * 4
        + [pl.BlockSpec(memory_space=pl.ANY)]
        + [pl.BlockSpec(memory_space=pltpu.VMEM)] * 2,
        scratch_shapes=[pltpu.VMEM((n0, n0), F32), pltpu.VMEM((rows, rows), F32)]
        + [pltpu.VMEM((1, n0), F32)] * 4
        + [pltpu.VMEM((8, B), F32), pltpu.SemaphoreType.DMA],
        compiler_params=pltpu.CompilerParams(vmem_limit_bytes=WIDE_VMEM),
        name="main_solve",
    )(mine, other, q_row, c_row, g, link, b_row)


def primal_kernel(tallies_ref, w_ref, d_ref, dual_ref, back_ref, y_ref, out_ref):
    held = tallies_ref[lax.axis_index("scen")]
    scale = d_ref[...].astype(F32)
    for slot, source in enumerate((dual_ref, back_ref)):
        dual = source[...]
        dual = jnp.where(held > slot, dual, jnp.zeros_like(dual))
        y_ref[slot : slot + 1, :] = dual
        out_ref[slot : slot + 1, :] = scale[slot : slot + 1] * mm(
            dual.astype(BF16), w_ref[slot]
        )


def primal(tallies, matrices, ratios, dual, back):
    return pl.pallas_call(
        primal_kernel,
        in_specs=[pl.BlockSpec(memory_space=pltpu.SMEM)]
        + [pl.BlockSpec(memory_space=pltpu.VMEM)] * 4,
        out_shape=(
            jax.ShapeDtypeStruct((2, dual.shape[1]), F32),
            jax.ShapeDtypeStruct(ratios.shape, F32),
        ),
        compiler_params=pltpu.CompilerParams(vmem_limit_bytes=VMEM),
        name="primal",
    )(tallies, matrices, ratios, dual, back)


def local(
    scen_size, col_size, matrices, ratios, damping, coupler, bounds, q_diag, c_vec, tallies
):
    n_s, n_z = scen_size, col_size
    rows = matrices.shape[1]
    n0 = coupler.shape[2]
    pos = lax.axis_index("scen")
    zpos = lax.axis_index("col")
    held = tallies[pos]
    own = held >= 1
    live = own | (tallies[pos ^ 1] == 2)
    partner = [(i, i ^ 1) for i in range(n_s)]

    def everyone(x, axis, count, **kw):
        return lax.all_to_all(
            jnp.broadcast_to(x[None], (count,) + x.shape), axis, 0, 0, **kw
        )

    gram1 = gram(1, n_z, matrices[1], ratios)
    later, gram1 = lax.optimization_barrier((matrices, gram1))
    gram_moved = lax.ppermute(gram1, "scen", partner)
    gram0 = gram(0, n_z, later[0], ratios)
    partial = jnp.where(own, gram0, gram_moved).astype(F16)
    partial, coupler, damping, bounds = lax.optimization_barrier(
        (partial, coupler, damping, bounds)
    )
    sides = [
        jnp.concatenate([coupler[k], damping[k : k + 1], bounds[k : k + 1]], axis=0)
        for k in range(2)
    ]
    side_moved = lax.ppermute(sides[1], "scen", partner)
    side = jnp.where(own, sides[0], side_moved)
    link = side[:rows]
    reg_row = side[rows : rows + 1].astype(F32)
    b_row = side[rows + 1 : rows + 2].astype(F32)
    share = n0 // n_z
    width = -(-(share + 1) // B) * B
    rhs = jnp.concatenate(
        [
            lax.dynamic_slice(link, (0, zpos * share), (rows, share)),
            side[rows + 1][:, None],
            jnp.zeros((rows, width - share - 1), BF16),
        ],
        axis=1,
    )
    rhs = jnp.where(live, rhs, jnp.zeros_like(rhs))

    received = lax.all_to_all(partial, "col", 0, 0).astype(F32)
    whole = everyone(jnp.sum(received, axis=0).astype(F16), "col", n_z)
    g, terms = solve(whole.astype(F32), reg_row, rhs, link)

    count = n_s // 2
    same = [[2 * i + k for i in range(count)] for k in range(2)]
    terms = terms.reshape((n_s,) + terms.shape[2:])
    mine = lax.all_to_all(terms, "scen", 0, 0, axis_index_groups=[same[0] + same[1]])
    wide = everyone(jnp.sum(mine, axis=0), "col", n_z)
    half = everyone(wide.astype(F16), "scen", count, axis_index_groups=same)
    other = lax.ppermute(half, "scen", partner)
    first, dual = main_solve(half.astype(F32), other.astype(F32), q_diag[None], c_vec[None], g, link, b_row)

    returned = lax.ppermute(dual, "scen", partner)
    duals, primals = primal(tallies, matrices, ratios, dual, returned)
    return first[0], duals, primals


def solution(mesh):
    body = functools.partial(local, mesh.shape["scen"], mesh.shape["col"])
    return jax.shard_map(
        body,
        mesh=mesh,
        in_specs=(
            P("scen", None, "col"),
            P("scen", "col"),
            P("scen", None),
            P("scen", None, None),
            P("scen", None),
            P(),
            P(),
            P(),
        ),
        out_specs=(P(), P("scen", None), P("scen", "col")),
        check_vma=False,
    )
```

```python
import functools

import jax
import jax.numpy as jnp
from jax import lax
from jax.experimental import pallas as pl
from jax.experimental.pallas import tpu as pltpu
from jax.sharding import PartitionSpec as P

F32 = jnp.float32
BF16 = jnp.bfloat16
F16 = jnp.float16
B = 128
TOL2 = 1e-10
MAX_STEPS = 4096
VMEM = 20 * 2**20
WIDE_VMEM = 50 * 2**20
SLABS = 16
RHO_SCALE = 0.25
STAGGER_NS = 1500


def blocks_of(rows):
    n = rows // B
    return [(i, j) for i in range(n) for j in range(i + 1)]


def mm(a, b):
    return lax.dot_general(a, b, (((1,), (0,)), ((), ())), preferred_element_type=F32)


def split3(x):
    hi = x.astype(BF16)
    rest = x - hi.astype(F32)
    mid = rest.astype(BF16)
    low = (rest - mid.astype(F32)).astype(BF16)
    return hi, mid, low


def eye_mask():
    return lax.broadcasted_iota(jnp.int32, (B, B), 0) == lax.broadcasted_iota(
        jnp.int32, (B, B), 1
    )


def gram_kernel(slot, parts, w_ref, d_ref, out_ref, scaled_ref, g_ref):
    if slot == 0:
        @pl.when(lax.rem(lax.axis_index("scen"), 2) == 1)
        def _():
            pl.delay(STAGGER_NS)

    rows = w_ref.shape[0]
    tiles = [slice(i * B, (i + 1) * B) for i in range(rows // B)]
    scale = d_ref[...].astype(F32)[slot : slot + 1]
    for at in tiles:
        scaled_ref[at, :] = (w_ref[at, :].astype(F32) * scale).astype(BF16)
    for at in tiles:
        g_ref[at, :] = lax.dot_general(
            scaled_ref[at, :], w_ref[...], (((1,), (1,)), ((), ())), preferred_element_type=F32
        )
    step = B // parts
    for b, (i, j) in enumerate(blocks_of(rows)):
        blk = g_ref[tiles[i], tiles[j]]
        if i != j:
            blk = 0.5 * (blk + g_ref[tiles[j], tiles[i]].T)
        for z in range(parts):
            out_ref[z, b * step : (b + 1) * step, :] = blk[z * step : (z + 1) * step, :]


def gram(slot, parts, matrix, ratios):
    rows, cols = matrix.shape
    height = len(blocks_of(rows)) * B // parts
    return pl.pallas_call(
        functools.partial(gram_kernel, slot, parts),
        out_shape=jax.ShapeDtypeStruct((parts, height, B), F32),
        scratch_shapes=[pltpu.VMEM((rows, cols), BF16), pltpu.VMEM((rows, rows), F32)],
        compiler_params=pltpu.CompilerParams(vmem_limit_bytes=VMEM),
        name=f"gram{slot}",
    )(matrix, ratios)


def choose_kernel(tallies_ref, own_ref, moved_ref, out_ref):
    held = tallies_ref[lax.axis_index("scen")]

    @pl.when(held >= 1)
    def _():
        out_ref[...] = own_ref[...]

    @pl.when(held < 1)
    def _():
        out_ref[...] = moved_ref[...]


def choose(tallies, own, moved):
    return pl.pallas_call(
        choose_kernel,
        in_specs=[pl.BlockSpec(memory_space=pltpu.SMEM)]
        + [pl.BlockSpec(memory_space=pltpu.VMEM)] * 2,
        out_shape=jax.ShapeDtypeStruct(own.shape, F32),
        compiler_params=pltpu.CompilerParams(vmem_limit_bytes=VMEM),
        name="choose",
    )(tallies, own, moved)


def ratio(a, b):
    ok = b > 0.0
    return jnp.where(ok, a / jnp.where(ok, b, 1.0), 0.0)


def low_lanes(shape):
    return lax.broadcasted_iota(jnp.int32, shape, len(shape) - 1) < B // 2


def cg_block(pieces, x_ref, r_ref, p_ref, s_ref, rb_ref, sc_ref):
    hi, mid = pieces
    rows = x_ref.shape[0]
    tiles = [slice(i * B, (i + 1) * B) for i in range(rows // B)]

    def body(carry):
        k, _ = carry
        rb = rb_ref[...]
        gamma, old, was, bound = (sc_ref[i : i + 1, :] for i in range(4))
        delta = jnp.zeros_like(gamma)
        for at in tiles:
            w = mm(hi[at, :], rb) + mm(mid[at, :], rb)
            x_ref[at, :] += was * p_ref[at, :]
            p_ref[at, :] = rb_ref[at, :].astype(F32) + ratio(gamma, old) * p_ref[at, :]
            s_ref[at, :] = w + ratio(gamma, old) * s_ref[at, :]
            delta += jnp.sum(p_ref[at, :] * s_ref[at, :], axis=0, keepdims=True)
        alpha = ratio(gamma, delta)
        new = jnp.zeros_like(gamma)
        size = jnp.zeros_like(gamma)
        for at in tiles:
            r = r_ref[at, :] - alpha * s_ref[at, :]
            r_ref[at, :] = r
            rounded = r.astype(BF16)
            rb_ref[at, :] = rounded
            new += jnp.sum(r * rounded.astype(F32), axis=0, keepdims=True)
        sc_ref[0:1, :] = new
        sc_ref[1:2, :] = gamma
        sc_ref[2:3, :] = alpha
        return k + 1, jnp.max(gamma - bound)

    rhs = r_ref[...]
    x_ref[...] = jnp.zeros_like(rhs)
    p_ref[...] = jnp.zeros_like(rhs)
    s_ref[...] = jnp.zeros_like(rhs)
    rounded = rhs.astype(BF16)
    rb_ref[...] = rounded
    first = jnp.sum(rhs * rounded.astype(F32), axis=0, keepdims=True)
    sc_ref[0:1, :] = first
    sc_ref[1:3, :] = jnp.zeros((2,) + first.shape[1:], F32)
    sc_ref[3:4, :] = TOL2 * first
    lax.while_loop(
        lambda c: (c[0] < MAX_STEPS) & (c[1] > 0.0), body, (jnp.int32(0), jnp.max(first))
    )
    for at in tiles:
        x_ref[at, :] += sc_ref[2:3, :] * p_ref[at, :]


def solve_kernel(
    recv_ref, reg_ref, rhs_ref, link_ref, g_hbm, out_ref,
    g_ref, hi_ref, mid_ref, x_ref, r_ref, p_ref, s_ref, rb_ref, sc_ref, sem,
):
    parts = recv_ref.shape[0]
    rows = g_ref.shape[0]
    step = B // parts
    eye = eye_mask()
    for b, (i, j) in enumerate(blocks_of(rows)):
        ri, rj = slice(i * B, (i + 1) * B), slice(j * B, (j + 1) * B)
        blk = jnp.concatenate(
            [recv_ref[z, b * step : (b + 1) * step, :] for z in range(parts)], axis=0
        )
        other = blk.T
        if i == j:
            blk = 0.5 * (blk + other) + jnp.where(eye, reg_ref[:, rj], 0.0)
        g_ref[ri, rj] = blk
        hi_ref[ri, rj], mid_ref[ri, rj] = split3(blk)[:2]
        if i != j:
            g_ref[rj, ri] = other
            hi_ref[rj, ri], mid_ref[rj, ri] = split3(other)[:2]
    keep = pltpu.make_async_copy(g_ref, g_hbm.at[0], sem)
    keep.start()
    r_ref[...] = rhs_ref[...].astype(F32)
    cg_block((hi_ref, mid_ref), x_ref, r_ref, p_ref, s_ref, rb_ref, sc_ref)
    n = x_ref.shape[1]
    pieces = jnp.concatenate(split3(x_ref[...]), axis=1)
    y = lax.dot_general(
        link_ref[...], pieces, (((0,), (0,)), ((), ())), preferred_element_type=F32
    )
    y = y[:, :n] + (y[:, n : 2 * n] + y[:, 2 * n :])
    half, quarter = B // 2, B // 4
    after = lax.rem(lax.axis_index("col") + 1, n0_blocks(rows))
    row = lax.broadcasted_iota(jnp.int32, y.shape, 0)
    lane = lax.broadcasted_iota(jnp.int32, y.shape, 1)
    start = after * half
    here = (row >= start) & (row < start + half) & (lane == 0)
    x_ref[...] = jnp.where(here, pltpu.roll(y, half, 1) * RHO_SCALE, y)
    low = low_lanes((quarter, B))
    for t in range(rows // B):
        for c in range(2):
            at = t * B + c * quarter
            up = pltpu.roll(x_ref[at + half : at + half + quarter, :], half, 1)
            out_ref[c, :, t, :] = jnp.where(low, x_ref[at : at + quarter, :], up)
    keep.wait()


def n0_blocks(rows):
    return rows // (B // 2)


def solve(received, reg_row, rhs, link):
    rows, width = rhs.shape
    return pl.pallas_call(
        solve_kernel,
        out_shape=(
            jax.ShapeDtypeStruct((SLABS, rows, rows), F32),
            jax.ShapeDtypeStruct((2, B // 4, rows // B, B), F32),
        ),
        in_specs=[pl.BlockSpec(memory_space=pltpu.VMEM)] * 4,
        out_specs=(
            pl.BlockSpec(memory_space=pl.ANY),
            pl.BlockSpec(memory_space=pltpu.VMEM),
        ),
        scratch_shapes=[pltpu.VMEM((rows, rows), F32)]
        + [pltpu.VMEM((rows, rows), BF16)] * 2
        + [pltpu.VMEM((rows, width), F32)] * 4
        + [pltpu.VMEM((rows, width), BF16), pltpu.VMEM((8, width), F32)]
        + [pltpu.SemaphoreType.DMA],
        compiler_params=pltpu.CompilerParams(vmem_limit_bytes=WIDE_VMEM),
        name="solve",
    )(received, reg_row, rhs, link)


def as_row(col, eye):
    return jnp.sum(jnp.where(eye, col, 0.0), axis=0, keepdims=True)


def as_col(row, eye):
    return jnp.sum(jnp.where(eye, row, 0.0), axis=1, keepdims=True)


def times_row(mat_ref, row, eye):
    rows = mat_ref.shape[0]
    out = []
    for i in range(rows // B):
        part = mat_ref[i * B : (i + 1) * B, :].astype(F32) * row
        out.append(as_row(jnp.sum(part, axis=1, keepdims=True), eye))
    return jnp.concatenate(out, axis=1)


def sym_times_row(mat_ref, row, eye):
    total = None
    for i in range(mat_ref.shape[0] // B):
        at = slice(i * B, (i + 1) * B)
        part = jnp.sum(mat_ref[at, :] * as_col(row[:, at], eye), axis=0, keepdims=True)
        total = part if total is None else total + part
    return total


def lane_sum(row):
    return jnp.sum(row, axis=1, keepdims=True)


def cg_row(mat_ref, rhs, x_ref, r_ref, p_ref, s_ref, sc_ref, eye):
    def body(carry):
        k, _ = carry
        old, bound, scale = (sc_ref[i : i + 1, 0:1] for i in range(3))
        r = r_ref[...]
        gamma = lane_sum(r * r)
        w = sym_times_row(mat_ref, r, eye)
        delta = lane_sum(r * w)
        beta = ratio(gamma, old)
        alpha = ratio(gamma, delta - beta * gamma * scale)
        p = r + beta * p_ref[...]
        s = w + beta * s_ref[...]
        p_ref[...] = p
        s_ref[...] = s
        x_ref[...] += alpha * p
        r_ref[...] = r - alpha * s
        sc_ref[0:1, 0:1] = gamma
        sc_ref[2:3, 0:1] = ratio(jnp.ones_like(alpha), alpha)
        return k + 1, jnp.max(gamma - bound)

    zero = jnp.zeros_like(rhs)
    x_ref[...] = zero
    p_ref[...] = zero
    s_ref[...] = zero
    r_ref[...] = rhs
    first = lane_sum(rhs * rhs)
    sc_ref[0:1, 0:1] = jnp.zeros_like(first)
    sc_ref[1:2, 0:1] = TOL2 * first
    sc_ref[2:3, 0:1] = jnp.zeros_like(first)
    lax.while_loop(
        lambda c: (c[0] < MAX_STEPS) & (c[1] > 0.0), body, (jnp.int32(0), jnp.max(first))
    )
    return x_ref[...]


def main_kernel(
    mine_ref, other_ref, q_ref, c_ref, g_hbm, link_ref, b_ref, first_ref, dual_ref,
    m_ref, g_ref, x_ref, r_ref, p_ref, s_ref, sc_ref, sem,
):
    load = pltpu.make_async_copy(g_hbm.at[0], g_ref, sem)
    load.start()
    quarter, shards, tiles, _ = mine_ref.shape
    half = 2 * quarter
    eye = eye_mask()
    core = lax.rem(lax.axis_index("scen"), 2)
    low = low_lanes((quarter, B))
    for src, which in ((mine_ref, core), (other_ref, 1 - core)):
        for t in range(tiles):
            top = pl.multiple_of(which * quarter + t * B, quarter)
            for m in range(shards // 2):
                v0, v1 = src[:, 2 * m, t, :], src[:, 2 * m + 1, t, :]
                at = slice(m * B, (m + 1) * B)
                m_ref[pl.ds(top, quarter), at] = jnp.where(low, v0, pltpu.roll(v1, half, 1))
                m_ref[pl.ds(top + half, quarter), at] = jnp.where(
                    low, pltpu.roll(v0, half, 1), v1
                )
    row = lax.broadcasted_iota(jnp.int32, (B, B), 0)
    lane = lax.broadcasted_iota(jnp.int32, (B, B), 1)
    rho = []
    for t in range(tiles):
        at = slice(t * B, (t + 1) * B)
        e = (t + tiles - 1) % tiles
        before = slice(e * B, (e + 1) * B)
        near, far = m_ref[at, at], m_ref[at, before]
        rho.append(as_row(jnp.where(row[:, :1] < half, far[:, half : half + 1], near[:, :1]), eye))
        give = jnp.where(
            lane[:1] < half,
            m_ref[e * B + half : e * B + half + 1, at],
            m_ref[t * B : t * B + 1, at],
        )
        give = as_col(give, eye)
        m_ref[at, at] = jnp.where((row >= half) & (lane == 0), give, near) + jnp.where(
            eye, q_ref[:, at], 0.0
        )
        m_ref[at, before] = jnp.where((row < half) & (lane == half), give, far)
    rhs = c_ref[...] - jnp.concatenate(rho, axis=1) * (1.0 / RHO_SCALE)
    refs = (x_ref, r_ref, p_ref, s_ref, sc_ref)
    first = cg_row(m_ref, rhs, *refs, eye)
    first_ref[...] = first
    pushed = b_ref[...] + times_row(link_ref, first, eye)
    load.wait()
    dual_ref[...] = cg_row(g_ref, pushed, *refs, eye)


def main_solve(mine, other, q_row, c_row, g, link, b_row):
    n0, rows = q_row.shape[1], b_row.shape[1]
    return pl.pallas_call(
        main_kernel,
        out_shape=(
            jax.ShapeDtypeStruct((1, n0), F32),
            jax.ShapeDtypeStruct((1, rows), F32),
        ),
        in_specs=[pl.BlockSpec(memory_space=pltpu.VMEM)] * 4
        + [pl.BlockSpec(memory_space=pl.ANY)]
        + [pl.BlockSpec(memory_space=pltpu.VMEM)] * 2,
        scratch_shapes=[pltpu.VMEM((n0, n0), F32), pltpu.VMEM((rows, rows), F32)]
        + [pltpu.VMEM((1, n0), F32)] * 4
        + [pltpu.VMEM((8, B), F32), pltpu.SemaphoreType.DMA],
        compiler_params=pltpu.CompilerParams(vmem_limit_bytes=WIDE_VMEM),
        name="main_solve",
    )(mine, other, q_row, c_row, g, link, b_row)


def primal_kernel(tallies_ref, w_ref, d_ref, dual_ref, back_ref, y_ref, out_ref):
    held = tallies_ref[lax.axis_index("scen")]
    scale = d_ref[...].astype(F32)
    for slot, source in enumerate((dual_ref, back_ref)):
        dual = source[...]
        dual = jnp.where(held > slot, dual, jnp.zeros_like(dual))
        y_ref[slot : slot + 1, :] = dual
        out_ref[slot : slot + 1, :] = scale[slot : slot + 1] * mm(
            dual.astype(BF16), w_ref[slot]
        )


def primal(tallies, matrices, ratios, dual, back):
    return pl.pallas_call(
        primal_kernel,
        in_specs=[pl.BlockSpec(memory_space=pltpu.SMEM)]
        + [pl.BlockSpec(memory_space=pltpu.VMEM)] * 4,
        out_shape=(
            jax.ShapeDtypeStruct((2, dual.shape[1]), F32),
            jax.ShapeDtypeStruct(ratios.shape, F32),
        ),
        compiler_params=pltpu.CompilerParams(vmem_limit_bytes=VMEM),
        name="primal",
    )(tallies, matrices, ratios, dual, back)


def local(
    scen_size, col_size, matrices, ratios, damping, coupler, bounds, q_diag, c_vec, tallies
):
    n_s, n_z = scen_size, col_size
    rows = matrices.shape[1]
    n0 = coupler.shape[2]
    pos = lax.axis_index("scen")
    zpos = lax.axis_index("col")
    held = tallies[pos]
    own = held >= 1
    live = own | (tallies[pos ^ 1] == 2)
    partner = [(i, i ^ 1) for i in range(n_s)]

    def everyone(x, axis, count, **kw):
        return lax.all_to_all(
            jnp.broadcast_to(x[None], (count,) + x.shape), axis, 0, 0, **kw
        )

    gram1 = gram(1, n_z, matrices[1], ratios)
    later, gram1 = lax.optimization_barrier((matrices, gram1))
    gram_moved = lax.ppermute(gram1, "scen", partner)
    gram0 = gram(0, n_z, later[0], ratios)
    partial = choose(tallies, gram0, gram_moved).astype(F16)
    partial, coupler, damping, bounds = lax.optimization_barrier(
        (partial, coupler, damping, bounds)
    )
    sides = [
        jnp.concatenate([coupler[k], damping[k : k + 1], bounds[k : k + 1]], axis=0)
        for k in range(2)
    ]
    side_moved = lax.ppermute(sides[1], "scen", partner)
    side = jnp.where(own, sides[0], side_moved)
    link = side[:rows]
    reg_row = side[rows : rows + 1].astype(F32)
    b_row = side[rows + 1 : rows + 2].astype(F32)
    share = n0 // n_z
    width = -(-(share + 1) // B) * B
    rhs = jnp.concatenate(
        [
            lax.dynamic_slice(link, (0, zpos * share), (rows, share)),
            side[rows + 1][:, None],
            jnp.zeros((rows, width - share - 1), BF16),
        ],
        axis=1,
    )
    rhs = jnp.where(live, rhs, jnp.zeros_like(rhs))

    received = lax.all_to_all(partial, "col", 0, 0).astype(F32)
    whole = everyone(jnp.sum(received, axis=0).astype(F16), "col", n_z)
    g, terms = solve(whole.astype(F32), reg_row, rhs, link)

    count = n_s // 2
    same = [[2 * i + k for i in range(count)] for k in range(2)]
    terms = terms.reshape((n_s,) + terms.shape[2:])
    mine = lax.all_to_all(terms, "scen", 0, 0, axis_index_groups=[same[0] + same[1]])
    wide = everyone(jnp.sum(mine, axis=0), "col", n_z)
    half = everyone(wide.astype(F16), "scen", count, axis_index_groups=same)
    other = lax.ppermute(half, "scen", partner)
    first, dual = main_solve(half.astype(F32), other.astype(F32), q_diag[None], c_vec[None], g, link, b_row)

    returned = lax.ppermute(dual, "scen", partner)
    duals, primals = primal(tallies, matrices, ratios, dual, returned)
    return first[0], duals, primals


def solution(mesh):
    body = functools.partial(local, mesh.shape["scen"], mesh.shape["col"])
    return jax.shard_map(
        body,
        mesh=mesh,
        in_specs=(
            P("scen", None, "col"),
            P("scen", "col"),
            P("scen", None),
            P("scen", None, None),
            P("scen", None),
            P(),
            P(),
            P(),
        ),
        out_specs=(P(), P("scen", None), P("scen", "col")),
        check_vma=False,
    )
```

```python
import functools

import jax
import jax.numpy as jnp
from jax import lax
from jax.experimental import pallas as pl
from jax.experimental.pallas import tpu as pltpu
from jax.sharding import PartitionSpec as P

F32 = jnp.float32
BF16 = jnp.bfloat16
F16 = jnp.float16
B = 128
TOL2 = 1e-10
MAX_STEPS = 4096
VMEM = 20 * 2**20
WIDE_VMEM = 50 * 2**20
SLABS = 16
RHO_SCALE = 0.25


def blocks_of(rows):
    n = rows // B
    return [(i, j) for i in range(n) for j in range(i + 1)]


def mm(a, b):
    return lax.dot_general(a, b, (((1,), (0,)), ((), ())), preferred_element_type=F32)


def split3(x):
    hi = x.astype(BF16)
    rest = x - hi.astype(F32)
    mid = rest.astype(BF16)
    low = (rest - mid.astype(F32)).astype(BF16)
    return hi, mid, low


def eye_mask():
    return lax.broadcasted_iota(jnp.int32, (B, B), 0) == lax.broadcasted_iota(
        jnp.int32, (B, B), 1
    )


def gram_kernel(slot, parts, w_ref, d_ref, out_ref, scaled_ref, g_ref):
    rows = w_ref.shape[0]
    tiles = [slice(i * B, (i + 1) * B) for i in range(rows // B)]
    scale = d_ref[...].astype(F32)[slot : slot + 1]
    for at in tiles:
        scaled_ref[at, :] = (w_ref[at, :].astype(F32) * scale).astype(BF16)
    for at in tiles:
        g_ref[at, :] = lax.dot_general(
            scaled_ref[at, :], w_ref[...], (((1,), (1,)), ((), ())), preferred_element_type=F32
        )
    step = B // parts
    for b, (i, j) in enumerate(blocks_of(rows)):
        blk = g_ref[tiles[i], tiles[j]]
        if i != j:
            blk = 0.5 * (blk + g_ref[tiles[j], tiles[i]].T)
        for z in range(parts):
            out_ref[z, b * step : (b + 1) * step, :] = blk[z * step : (z + 1) * step, :]


def gram(slot, parts, matrix, ratios):
    rows, cols = matrix.shape
    height = len(blocks_of(rows)) * B // parts
    return pl.pallas_call(
        functools.partial(gram_kernel, slot, parts),
        out_shape=jax.ShapeDtypeStruct((parts, height, B), F32),
        scratch_shapes=[pltpu.VMEM((rows, cols), BF16), pltpu.VMEM((rows, rows), F32)],
        compiler_params=pltpu.CompilerParams(vmem_limit_bytes=VMEM),
        name=f"gram{slot}",
    )(matrix, ratios)


def choose_kernel(tallies_ref, own_ref, moved_ref, out_ref):
    held = tallies_ref[lax.axis_index("scen")]

    @pl.when(held >= 1)
    def _():
        out_ref[...] = own_ref[...]

    @pl.when(held < 1)
    def _():
        out_ref[...] = moved_ref[...]


def choose(tallies, own, moved):
    return pl.pallas_call(
        choose_kernel,
        in_specs=[pl.BlockSpec(memory_space=pltpu.SMEM)]
        + [pl.BlockSpec(memory_space=pltpu.VMEM)] * 2,
        out_shape=jax.ShapeDtypeStruct(own.shape, F32),
        compiler_params=pltpu.CompilerParams(vmem_limit_bytes=VMEM),
        name="choose",
    )(tallies, own, moved)


def ratio(a, b):
    ok = b > 0.0
    return jnp.where(ok, a / jnp.where(ok, b, 1.0), 0.0)


def low_lanes(shape):
    return lax.broadcasted_iota(jnp.int32, shape, len(shape) - 1) < B // 2


def cg_block(pieces, x_ref, r_ref, p_ref, s_ref, rb_ref, sc_ref):
    hi, mid = pieces
    rows = x_ref.shape[0]
    tiles = [slice(i * B, (i + 1) * B) for i in range(rows // B)]

    def body(carry):
        k, _ = carry
        rb = rb_ref[...]
        gamma, old, was, bound = (sc_ref[i : i + 1, :] for i in range(4))
        delta = jnp.zeros_like(gamma)
        for at in tiles:
            w = mm(hi[at, :], rb) + mm(mid[at, :], rb)
            x_ref[at, :] += was * p_ref[at, :]
            p_ref[at, :] = rb_ref[at, :].astype(F32) + ratio(gamma, old) * p_ref[at, :]
            s_ref[at, :] = w + ratio(gamma, old) * s_ref[at, :]
            delta += jnp.sum(p_ref[at, :] * s_ref[at, :], axis=0, keepdims=True)
        alpha = ratio(gamma, delta)
        new = jnp.zeros_like(gamma)
        size = jnp.zeros_like(gamma)
        for at in tiles:
            r = r_ref[at, :] - alpha * s_ref[at, :]
            r_ref[at, :] = r
            rounded = r.astype(BF16)
            rb_ref[at, :] = rounded
            new += jnp.sum(r * rounded.astype(F32), axis=0, keepdims=True)
        sc_ref[0:1, :] = new
        sc_ref[1:2, :] = gamma
        sc_ref[2:3, :] = alpha
        return k + 1, jnp.max(gamma - bound)

    rhs = r_ref[...]
    x_ref[...] = jnp.zeros_like(rhs)
    p_ref[...] = jnp.zeros_like(rhs)
    s_ref[...] = jnp.zeros_like(rhs)
    rounded = rhs.astype(BF16)
    rb_ref[...] = rounded
    first = jnp.sum(rhs * rounded.astype(F32), axis=0, keepdims=True)
    sc_ref[0:1, :] = first
    sc_ref[1:3, :] = jnp.zeros((2,) + first.shape[1:], F32)
    sc_ref[3:4, :] = TOL2 * first
    lax.while_loop(
        lambda c: (c[0] < MAX_STEPS) & (c[1] > 0.0), body, (jnp.int32(0), jnp.max(first))
    )
    for at in tiles:
        x_ref[at, :] += sc_ref[2:3, :] * p_ref[at, :]


def solve_kernel(
    recv_ref, reg_ref, rhs_ref, link_ref, g_hbm, out_ref,
    g_ref, hi_ref, mid_ref, x_ref, r_ref, p_ref, s_ref, rb_ref, sc_ref, sem,
):
    parts = recv_ref.shape[0]
    rows = g_ref.shape[0]
    step = B // parts
    eye = eye_mask()
    for b, (i, j) in enumerate(blocks_of(rows)):
        ri, rj = slice(i * B, (i + 1) * B), slice(j * B, (j + 1) * B)
        blk = jnp.concatenate(
            [recv_ref[z, b * step : (b + 1) * step, :] for z in range(parts)], axis=0
        )
        other = blk.T
        if i == j:
            blk = 0.5 * (blk + other) + jnp.where(eye, reg_ref[:, rj], 0.0)
        g_ref[ri, rj] = blk
        hi_ref[ri, rj], mid_ref[ri, rj] = split3(blk)[:2]
        if i != j:
            g_ref[rj, ri] = other
            hi_ref[rj, ri], mid_ref[rj, ri] = split3(other)[:2]
    keep = pltpu.make_async_copy(g_ref, g_hbm.at[0], sem)
    keep.start()
    r_ref[...] = rhs_ref[...].astype(F32)
    cg_block((hi_ref, mid_ref), x_ref, r_ref, p_ref, s_ref, rb_ref, sc_ref)
    n = x_ref.shape[1]
    pieces = jnp.concatenate(split3(x_ref[...]), axis=1)
    y = lax.dot_general(
        link_ref[...], pieces, (((0,), (0,)), ((), ())), preferred_element_type=F32
    )
    y = y[:, :n] + (y[:, n : 2 * n] + y[:, 2 * n :])
    half, quarter = B // 2, B // 4
    after = lax.rem(lax.axis_index("col") + 1, n0_blocks(rows))
    row = lax.broadcasted_iota(jnp.int32, y.shape, 0)
    lane = lax.broadcasted_iota(jnp.int32, y.shape, 1)
    start = after * half
    here = (row >= start) & (row < start + half) & (lane == 0)
    x_ref[...] = jnp.where(here, pltpu.roll(y, half, 1) * RHO_SCALE, y)
    low = low_lanes((quarter, B))
    for t in range(rows // B):
        for c in range(2):
            at = t * B + c * quarter
            up = pltpu.roll(x_ref[at + half : at + half + quarter, :], half, 1)
            out_ref[c, :, t, :] = jnp.where(low, x_ref[at : at + quarter, :], up)
    keep.wait()


def n0_blocks(rows):
    return rows // (B // 2)


def solve(received, reg_row, rhs, link):
    rows, width = rhs.shape
    return pl.pallas_call(
        solve_kernel,
        out_shape=(
            jax.ShapeDtypeStruct((SLABS, rows, rows), F32),
            jax.ShapeDtypeStruct((2, B // 4, rows // B, B), F32),
        ),
        in_specs=[pl.BlockSpec(memory_space=pltpu.VMEM)] * 4,
        out_specs=(
            pl.BlockSpec(memory_space=pl.ANY),
            pl.BlockSpec(memory_space=pltpu.VMEM),
        ),
        scratch_shapes=[pltpu.VMEM((rows, rows), F32)]
        + [pltpu.VMEM((rows, rows), BF16)] * 2
        + [pltpu.VMEM((rows, width), F32)] * 4
        + [pltpu.VMEM((rows, width), BF16), pltpu.VMEM((8, width), F32)]
        + [pltpu.SemaphoreType.DMA],
        compiler_params=pltpu.CompilerParams(vmem_limit_bytes=WIDE_VMEM),
        name="solve",
    )(received, reg_row, rhs, link)


def as_row(col, eye):
    return jnp.sum(jnp.where(eye, col, 0.0), axis=0, keepdims=True)


def as_col(row, eye):
    return jnp.sum(jnp.where(eye, row, 0.0), axis=1, keepdims=True)


def times_row(mat_ref, row, eye):
    rows = mat_ref.shape[0]
    out = []
    for i in range(rows // B):
        part = mat_ref[i * B : (i + 1) * B, :].astype(F32) * row
        out.append(as_row(jnp.sum(part, axis=1, keepdims=True), eye))
    return jnp.concatenate(out, axis=1)


def sym_times_row(mat_ref, row, eye):
    total = None
    for i in range(mat_ref.shape[0] // B):
        at = slice(i * B, (i + 1) * B)
        part = jnp.sum(mat_ref[at, :] * as_col(row[:, at], eye), axis=0, keepdims=True)
        total = part if total is None else total + part
    return total


def lane_sum(row):
    return jnp.sum(row, axis=1, keepdims=True)


def cg_row(mat_ref, rhs, x_ref, r_ref, p_ref, s_ref, sc_ref, eye):
    def body(carry):
        k, _ = carry
        old, bound, scale = (sc_ref[i : i + 1, 0:1] for i in range(3))
        r = r_ref[...]
        gamma = lane_sum(r * r)
        w = sym_times_row(mat_ref, r, eye)
        delta = lane_sum(r * w)
        beta = ratio(gamma, old)
        alpha = ratio(gamma, delta - beta * gamma * scale)
        p = r + beta * p_ref[...]
        s = w + beta * s_ref[...]
        p_ref[...] = p
        s_ref[...] = s
        x_ref[...] += alpha * p
        r_ref[...] = r - alpha * s
        sc_ref[0:1, 0:1] = gamma
        sc_ref[2:3, 0:1] = ratio(jnp.ones_like(alpha), alpha)
        return k + 1, jnp.max(gamma - bound)

    zero = jnp.zeros_like(rhs)
    x_ref[...] = zero
    p_ref[...] = zero
    s_ref[...] = zero
    r_ref[...] = rhs
    first = lane_sum(rhs * rhs)
    sc_ref[0:1, 0:1] = jnp.zeros_like(first)
    sc_ref[1:2, 0:1] = TOL2 * first
    sc_ref[2:3, 0:1] = jnp.zeros_like(first)
    lax.while_loop(
        lambda c: (c[0] < MAX_STEPS) & (c[1] > 0.0), body, (jnp.int32(0), jnp.max(first))
    )
    return x_ref[...]


def main_kernel(
    mine_ref, other_ref, q_ref, c_ref, g_hbm, link_ref, b_ref, first_ref, dual_ref,
    m_ref, g_ref, x_ref, r_ref, p_ref, s_ref, sc_ref, sem,
):
    load = pltpu.make_async_copy(g_hbm.at[0], g_ref, sem)
    load.start()
    quarter, shards, tiles, _ = mine_ref.shape
    half = 2 * quarter
    eye = eye_mask()
    core = lax.rem(lax.axis_index("scen"), 2)
    low = low_lanes((quarter, B))
    for src, which in ((mine_ref, core), (other_ref, 1 - core)):
        for t in range(tiles):
            top = pl.multiple_of(which * quarter + t * B, quarter)
            for m in range(shards // 2):
                v0, v1 = src[:, 2 * m, t, :], src[:, 2 * m + 1, t, :]
                at = slice(m * B, (m + 1) * B)
                m_ref[pl.ds(top, quarter), at] = jnp.where(low, v0, pltpu.roll(v1, half, 1))
                m_ref[pl.ds(top + half, quarter), at] = jnp.where(
                    low, pltpu.roll(v0, half, 1), v1
                )
    row = lax.broadcasted_iota(jnp.int32, (B, B), 0)
    lane = lax.broadcasted_iota(jnp.int32, (B, B), 1)
    rho = []
    for t in range(tiles):
        at = slice(t * B, (t + 1) * B)
        e = (t + tiles - 1) % tiles
        before = slice(e * B, (e + 1) * B)
        near, far = m_ref[at, at], m_ref[at, before]
        rho.append(as_row(jnp.where(row[:, :1] < half, far[:, half : half + 1], near[:, :1]), eye))
        give = jnp.where(
            lane[:1] < half,
            m_ref[e * B + half : e * B + half + 1, at],
            m_ref[t * B : t * B + 1, at],
        )
        give = as_col(give, eye)
        m_ref[at, at] = jnp.where((row >= half) & (lane == 0), give, near) + jnp.where(
            eye, q_ref[:, at], 0.0
        )
        m_ref[at, before] = jnp.where((row < half) & (lane == half), give, far)
    rhs = c_ref[...] - jnp.concatenate(rho, axis=1) * (1.0 / RHO_SCALE)
    refs = (x_ref, r_ref, p_ref, s_ref, sc_ref)
    first = cg_row(m_ref, rhs, *refs, eye)
    first_ref[...] = first
    pushed = b_ref[...] + times_row(link_ref, first, eye)
    load.wait()
    dual_ref[...] = cg_row(g_ref, pushed, *refs, eye)


def main_solve(mine, other, q_row, c_row, g, link, b_row):
    n0, rows = q_row.shape[1], b_row.shape[1]
    return pl.pallas_call(
        main_kernel,
        out_shape=(
            jax.ShapeDtypeStruct((1, n0), F32),
            jax.ShapeDtypeStruct((1, rows), F32),
        ),
        in_specs=[pl.BlockSpec(memory_space=pltpu.VMEM)] * 4
        + [pl.BlockSpec(memory_space=pl.ANY)]
        + [pl.BlockSpec(memory_space=pltpu.VMEM)] * 2,
        scratch_shapes=[pltpu.VMEM((n0, n0), F32), pltpu.VMEM((rows, rows), F32)]
        + [pltpu.VMEM((1, n0), F32)] * 4
        + [pltpu.VMEM((8, B), F32), pltpu.SemaphoreType.DMA],
        compiler_params=pltpu.CompilerParams(vmem_limit_bytes=WIDE_VMEM),
        name="main_solve",
    )(mine, other, q_row, c_row, g, link, b_row)


def primal_kernel(tallies_ref, w_ref, d_ref, dual_ref, back_ref, y_ref, out_ref):
    held = tallies_ref[lax.axis_index("scen")]
    scale = d_ref[...].astype(F32)
    for slot, source in enumerate((dual_ref, back_ref)):
        dual = source[...]
        dual = jnp.where(held > slot, dual, jnp.zeros_like(dual))
        y_ref[slot : slot + 1, :] = dual
        out_ref[slot : slot + 1, :] = scale[slot : slot + 1] * mm(
            dual.astype(BF16), w_ref[slot]
        )


def primal(tallies, matrices, ratios, dual, back):
    return pl.pallas_call(
        primal_kernel,
        in_specs=[pl.BlockSpec(memory_space=pltpu.SMEM)]
        + [pl.BlockSpec(memory_space=pltpu.VMEM)] * 4,
        out_shape=(
            jax.ShapeDtypeStruct((2, dual.shape[1]), F32),
            jax.ShapeDtypeStruct(ratios.shape, F32),
        ),
        compiler_params=pltpu.CompilerParams(vmem_limit_bytes=VMEM),
        name="primal",
    )(tallies, matrices, ratios, dual, back)


def local(
    scen_size, col_size, matrices, ratios, damping, coupler, bounds, q_diag, c_vec, tallies
):
    n_s, n_z = scen_size, col_size
    rows = matrices.shape[1]
    n0 = coupler.shape[2]
    pos = lax.axis_index("scen")
    zpos = lax.axis_index("col")
    held = tallies[pos]
    own = held >= 1
    live = own | (tallies[pos ^ 1] == 2)
    partner = [(i, i ^ 1) for i in range(n_s)]

    def everyone(x, axis, count, **kw):
        return lax.all_to_all(
            jnp.broadcast_to(x[None], (count,) + x.shape), axis, 0, 0, **kw
        )

    gram1 = gram(1, n_z, matrices[1], ratios)
    later, gram1 = lax.optimization_barrier((matrices, gram1))
    gram_moved = lax.ppermute(gram1, "scen", partner)
    gram0 = gram(0, n_z, later[0], ratios)
    partial = choose(tallies, gram0, gram_moved).astype(F16)
    partial, coupler, damping, bounds = lax.optimization_barrier(
        (partial, coupler, damping, bounds)
    )
    sides = [
        jnp.concatenate([coupler[k], damping[k : k + 1], bounds[k : k + 1]], axis=0)
        for k in range(2)
    ]
    side_moved = lax.ppermute(sides[1], "scen", partner)
    side = jnp.where(own, sides[0], side_moved)
    link = side[:rows]
    reg_row = side[rows : rows + 1].astype(F32)
    b_row = side[rows + 1 : rows + 2].astype(F32)
    share = n0 // n_z
    width = -(-(share + 1) // B) * B
    rhs = jnp.concatenate(
        [
            lax.dynamic_slice(link, (0, zpos * share), (rows, share)),
            side[rows + 1][:, None],
            jnp.zeros((rows, width - share - 1), BF16),
        ],
        axis=1,
    )
    rhs = jnp.where(live, rhs, jnp.zeros_like(rhs))

    received = lax.all_to_all(partial, "col", 0, 0).astype(F32)
    whole = everyone(jnp.sum(received, axis=0).astype(F16), "col", n_z)
    g, terms = solve(whole.astype(F32), reg_row, rhs, link)

    count = n_s // 2
    same = [[2 * i + k for i in range(count)] for k in range(2)]
    terms = terms.reshape((n_s,) + terms.shape[2:])
    mine = lax.all_to_all(terms, "scen", 0, 0, axis_index_groups=[same[0] + same[1]])
    rows_of = [[k * n_z + z for k in group for z in range(n_z)] for group in same]
    half = everyone(
        jnp.sum(mine, axis=0).astype(F16), ("scen", "col"), count * n_z, axis_index_groups=rows_of
    )
    half = half.reshape((count, n_z) + half.shape[1:])
    other = lax.ppermute(half, "scen", partner)
    first, dual = main_solve(half.astype(F32), other.astype(F32), q_diag[None], c_vec[None], g, link, b_row)

    returned = lax.ppermute(dual, "scen", partner)
    duals, primals = primal(tallies, matrices, ratios, dual, returned)
    return first[0], duals, primals


def solution(mesh):
    body = functools.partial(local, mesh.shape["scen"], mesh.shape["col"])
    return jax.shard_map(
        body,
        mesh=mesh,
        in_specs=(
            P("scen", None, "col"),
            P("scen", "col"),
            P("scen", None),
            P("scen", None, None),
            P("scen", None),
            P(),
            P(),
            P(),
        ),
        out_specs=(P(), P("scen", None), P("scen", "col")),
        check_vma=False,
    )
```

```python
import functools

import jax
import jax.numpy as jnp
from jax import lax
from jax.experimental import pallas as pl
from jax.experimental.pallas import tpu as pltpu
from jax.sharding import PartitionSpec as P

F32 = jnp.float32
BF16 = jnp.bfloat16
F16 = jnp.float16
B = 128
TOL2 = 1e-10
MAX_STEPS = 4096
VMEM = 20 * 2**20
WIDE_VMEM = 50 * 2**20
SLABS = 16
RHO_SCALE = 0.25


def blocks_of(rows):
    n = rows // B
    return [(i, j) for i in range(n) for j in range(i + 1)]


def mm(a, b):
    return lax.dot_general(a, b, (((1,), (0,)), ((), ())), preferred_element_type=F32)


def split3(x):
    hi = x.astype(BF16)
    rest = x - hi.astype(F32)
    mid = rest.astype(BF16)
    low = (rest - mid.astype(F32)).astype(BF16)
    return hi, mid, low


def eye_mask():
    return lax.broadcasted_iota(jnp.int32, (B, B), 0) == lax.broadcasted_iota(
        jnp.int32, (B, B), 1
    )


def gram_kernel(slot, parts, w_ref, d_ref, out_ref, scaled_ref, g_ref):
    rows = w_ref.shape[0]
    tiles = [slice(i * B, (i + 1) * B) for i in range(rows // B)]
    scale = d_ref[...].astype(F32)[slot : slot + 1]
    for at in tiles:
        scaled_ref[at, :] = (w_ref[at, :].astype(F32) * scale).astype(BF16)
    for at in tiles:
        g_ref[at, :] = lax.dot_general(
            scaled_ref[at, :], w_ref[...], (((1,), (1,)), ((), ())), preferred_element_type=F32
        )
    step = B // parts
    for b, (i, j) in enumerate(blocks_of(rows)):
        blk = g_ref[tiles[i], tiles[j]]
        if i != j:
            blk = 0.5 * (blk + g_ref[tiles[j], tiles[i]].T)
        for z in range(parts):
            out_ref[z, b * step : (b + 1) * step, :] = blk[z * step : (z + 1) * step, :]


def gram(slot, parts, matrix, ratios):
    rows, cols = matrix.shape
    height = len(blocks_of(rows)) * B // parts
    return pl.pallas_call(
        functools.partial(gram_kernel, slot, parts),
        out_shape=jax.ShapeDtypeStruct((parts, height, B), F32),
        scratch_shapes=[pltpu.VMEM((rows, cols), BF16), pltpu.VMEM((rows, rows), F32)],
        compiler_params=pltpu.CompilerParams(vmem_limit_bytes=VMEM),
        name=f"gram{slot}",
    )(matrix, ratios)


def choose_kernel(tallies_ref, own_ref, moved_ref, out_ref):
    held = tallies_ref[lax.axis_index("scen")]

    @pl.when(held >= 1)
    def _():
        out_ref[...] = own_ref[...]

    @pl.when(held < 1)
    def _():
        out_ref[...] = moved_ref[...]


def choose(tallies, own, moved):
    return pl.pallas_call(
        choose_kernel,
        in_specs=[pl.BlockSpec(memory_space=pltpu.SMEM)]
        + [pl.BlockSpec(memory_space=pltpu.VMEM)] * 2,
        out_shape=jax.ShapeDtypeStruct(own.shape, F32),
        compiler_params=pltpu.CompilerParams(vmem_limit_bytes=VMEM),
        name="choose",
    )(tallies, own, moved)


def ratio(a, b):
    ok = b > 0.0
    return jnp.where(ok, a / jnp.where(ok, b, 1.0), 0.0)


def low_lanes(shape):
    return lax.broadcasted_iota(jnp.int32, shape, len(shape) - 1) < B // 2


def cg_block(pieces, x_ref, r_ref, p_ref, s_ref, rb_ref, sc_ref):
    hi, mid = pieces
    rows = x_ref.shape[0]
    tiles = [slice(i * B, (i + 1) * B) for i in range(rows // B)]

    def body(carry):
        k, _ = carry
        rb = rb_ref[...]
        gamma, old, was, bound = (sc_ref[i : i + 1, :] for i in range(4))
        delta = jnp.zeros_like(gamma)
        for at in tiles:
            w = mm(hi[at, :], rb) + mm(mid[at, :], rb)
            x_ref[at, :] += was * p_ref[at, :]
            p_ref[at, :] = rb_ref[at, :].astype(F32) + ratio(gamma, old) * p_ref[at, :]
            s_ref[at, :] = w + ratio(gamma, old) * s_ref[at, :]
            delta += jnp.sum(p_ref[at, :] * s_ref[at, :], axis=0, keepdims=True)
        alpha = ratio(gamma, delta)
        new = jnp.zeros_like(gamma)
        size = jnp.zeros_like(gamma)
        for at in tiles:
            r = r_ref[at, :] - alpha * s_ref[at, :]
            r_ref[at, :] = r
            rounded = r.astype(BF16)
            rb_ref[at, :] = rounded
            new += jnp.sum(r * rounded.astype(F32), axis=0, keepdims=True)
        sc_ref[0:1, :] = new
        sc_ref[1:2, :] = gamma
        sc_ref[2:3, :] = alpha
        return k + 1, jnp.max(gamma - bound)

    rhs = r_ref[...]
    x_ref[...] = jnp.zeros_like(rhs)
    p_ref[...] = jnp.zeros_like(rhs)
    s_ref[...] = jnp.zeros_like(rhs)
    rounded = rhs.astype(BF16)
    rb_ref[...] = rounded
    first = jnp.sum(rhs * rounded.astype(F32), axis=0, keepdims=True)
    sc_ref[0:1, :] = first
    sc_ref[1:3, :] = jnp.zeros((2,) + first.shape[1:], F32)
    sc_ref[3:4, :] = TOL2 * first
    lax.while_loop(
        lambda c: (c[0] < MAX_STEPS) & (c[1] > 0.0), body, (jnp.int32(0), jnp.max(first))
    )
    for at in tiles:
        x_ref[at, :] += sc_ref[2:3, :] * p_ref[at, :]


def solve_kernel(
    recv_ref, reg_ref, rhs_ref, link_ref, g_hbm, out_ref,
    g_ref, hi_ref, mid_ref, x_ref, r_ref, p_ref, s_ref, rb_ref, sc_ref, sem,
):
    parts = recv_ref.shape[0]
    rows = g_ref.shape[0]
    step = B // parts
    eye = eye_mask()
    for b, (i, j) in enumerate(blocks_of(rows)):
        ri, rj = slice(i * B, (i + 1) * B), slice(j * B, (j + 1) * B)
        blk = jnp.concatenate(
            [recv_ref[z, b * step : (b + 1) * step, :] for z in range(parts)], axis=0
        )
        other = blk.T
        if i == j:
            blk = 0.5 * (blk + other) + jnp.where(eye, reg_ref[:, rj], 0.0)
        g_ref[ri, rj] = blk
        hi_ref[ri, rj], mid_ref[ri, rj] = split3(blk)[:2]
        if i != j:
            g_ref[rj, ri] = other
            hi_ref[rj, ri], mid_ref[rj, ri] = split3(other)[:2]
    keep = pltpu.make_async_copy(g_ref, g_hbm.at[0], sem)
    keep.start()
    r_ref[...] = rhs_ref[...].astype(F32)
    cg_block((hi_ref, mid_ref), x_ref, r_ref, p_ref, s_ref, rb_ref, sc_ref)
    n = x_ref.shape[1]
    pieces = jnp.concatenate(split3(x_ref[...]), axis=1)
    y = lax.dot_general(
        link_ref[...], pieces, (((0,), (0,)), ((), ())), preferred_element_type=F32
    )
    y = y[:, :n] + (y[:, n : 2 * n] + y[:, 2 * n :])
    half, quarter = B // 2, B // 4
    after = lax.rem(lax.axis_index("col") + 1, n0_blocks(rows))
    row = lax.broadcasted_iota(jnp.int32, y.shape, 0)
    lane = lax.broadcasted_iota(jnp.int32, y.shape, 1)
    start = after * half
    here = (row >= start) & (row < start + half) & (lane == 0)
    x_ref[...] = jnp.where(here, pltpu.roll(y, half, 1) * RHO_SCALE, y)
    low = low_lanes((quarter, B))
    for t in range(rows // B):
        for c in range(2):
            at = t * B + c * quarter
            up = pltpu.roll(x_ref[at + half : at + half + quarter, :], half, 1)
            out_ref[c, :, t, :] = jnp.where(low, x_ref[at : at + quarter, :], up)
    keep.wait()


def n0_blocks(rows):
    return rows // (B // 2)


def solve(received, reg_row, rhs, link):
    rows, width = rhs.shape
    return pl.pallas_call(
        solve_kernel,
        out_shape=(
            jax.ShapeDtypeStruct((SLABS, rows, rows), F32),
            jax.ShapeDtypeStruct((2, B // 4, rows // B, B), F32),
        ),
        in_specs=[pl.BlockSpec(memory_space=pltpu.VMEM)] * 4,
        out_specs=(
            pl.BlockSpec(memory_space=pl.ANY),
            pl.BlockSpec(memory_space=pltpu.VMEM),
        ),
        scratch_shapes=[pltpu.VMEM((rows, rows), F32)]
        + [pltpu.VMEM((rows, rows), BF16)] * 2
        + [pltpu.VMEM((rows, width), F32)] * 4
        + [pltpu.VMEM((rows, width), BF16), pltpu.VMEM((8, width), F32)]
        + [pltpu.SemaphoreType.DMA],
        compiler_params=pltpu.CompilerParams(vmem_limit_bytes=WIDE_VMEM),
        name="solve",
    )(received, reg_row, rhs, link)


def as_row(col, eye):
    return jnp.sum(jnp.where(eye, col, 0.0), axis=0, keepdims=True)


def as_col(row, eye):
    return jnp.sum(jnp.where(eye, row, 0.0), axis=1, keepdims=True)


def times_row(mat_ref, row, eye):
    rows = mat_ref.shape[0]
    out = []
    for i in range(rows // B):
        part = mat_ref[i * B : (i + 1) * B, :].astype(F32) * row
        out.append(as_row(jnp.sum(part, axis=1, keepdims=True), eye))
    return jnp.concatenate(out, axis=1)


def sym_times_row(mat_ref, row, eye):
    total = None
    for i in range(mat_ref.shape[0] // B):
        at = slice(i * B, (i + 1) * B)
        part = jnp.sum(mat_ref[at, :] * as_col(row[:, at], eye), axis=0, keepdims=True)
        total = part if total is None else total + part
    return total


def lane_sum(row):
    return jnp.sum(row, axis=1, keepdims=True)


def cg_row(mat_ref, rhs, x_ref, r_ref, p_ref, s_ref, sc_ref, eye):
    def body(carry):
        k, _ = carry
        old, bound, scale = (sc_ref[i : i + 1, 0:1] for i in range(3))
        r = r_ref[...]
        gamma = lane_sum(r * r)
        w = sym_times_row(mat_ref, r, eye)
        delta = lane_sum(r * w)
        beta = ratio(gamma, old)
        alpha = ratio(gamma, delta - beta * gamma * scale)
        p = r + beta * p_ref[...]
        s = w + beta * s_ref[...]
        p_ref[...] = p
        s_ref[...] = s
        x_ref[...] += alpha * p
        r_ref[...] = r - alpha * s
        sc_ref[0:1, 0:1] = gamma
        sc_ref[2:3, 0:1] = ratio(jnp.ones_like(alpha), alpha)
        return k + 1, jnp.max(gamma - bound)

    zero = jnp.zeros_like(rhs)
    x_ref[...] = zero
    p_ref[...] = zero
    s_ref[...] = zero
    r_ref[...] = rhs
    first = lane_sum(rhs * rhs)
    sc_ref[0:1, 0:1] = jnp.zeros_like(first)
    sc_ref[1:2, 0:1] = TOL2 * first
    sc_ref[2:3, 0:1] = jnp.zeros_like(first)
    lax.while_loop(
        lambda c: (c[0] < MAX_STEPS) & (c[1] > 0.0), body, (jnp.int32(0), jnp.max(first))
    )
    return x_ref[...]


def main_kernel(
    mine_ref, other_ref, q_ref, c_ref, g_hbm, link_ref, b_ref, first_ref, dual_ref,
    m_ref, g_ref, x_ref, r_ref, p_ref, s_ref, sc_ref, sem,
):
    load = pltpu.make_async_copy(g_hbm.at[0], g_ref, sem)
    load.start()
    quarter, shards, tiles, _ = mine_ref.shape
    half = 2 * quarter
    eye = eye_mask()
    core = lax.rem(lax.axis_index("scen"), 2)
    low = low_lanes((quarter, B))
    for src, which in ((mine_ref, core), (other_ref, 1 - core)):
        for t in range(tiles):
            top = pl.multiple_of(which * quarter + t * B, quarter)
            for m in range(shards // 2):
                v0, v1 = src[:, 2 * m, t, :], src[:, 2 * m + 1, t, :]
                at = slice(m * B, (m + 1) * B)
                m_ref[pl.ds(top, quarter), at] = jnp.where(low, v0, pltpu.roll(v1, half, 1))
                m_ref[pl.ds(top + half, quarter), at] = jnp.where(
                    low, pltpu.roll(v0, half, 1), v1
                )
    row = lax.broadcasted_iota(jnp.int32, (B, B), 0)
    lane = lax.broadcasted_iota(jnp.int32, (B, B), 1)
    rho = []
    for t in range(tiles):
        at = slice(t * B, (t + 1) * B)
        e = (t + tiles - 1) % tiles
        before = slice(e * B, (e + 1) * B)
        near, far = m_ref[at, at], m_ref[at, before]
        rho.append(as_row(jnp.where(row[:, :1] < half, far[:, half : half + 1], near[:, :1]), eye))
        give = jnp.where(
            lane[:1] < half,
            m_ref[e * B + half : e * B + half + 1, at],
            m_ref[t * B : t * B + 1, at],
        )
        give = as_col(give, eye)
        m_ref[at, at] = jnp.where((row >= half) & (lane == 0), give, near) + jnp.where(
            eye, q_ref[:, at], 0.0
        )
        m_ref[at, before] = jnp.where((row < half) & (lane == half), give, far)
    rhs = c_ref[...] - jnp.concatenate(rho, axis=1) * (1.0 / RHO_SCALE)
    refs = (x_ref, r_ref, p_ref, s_ref, sc_ref)
    first = cg_row(m_ref, rhs, *refs, eye)
    first_ref[...] = first
    pushed = b_ref[...] + times_row(link_ref, first, eye)
    load.wait()
    dual_ref[...] = cg_row(g_ref, pushed, *refs, eye)


def main_solve(mine, other, q_row, c_row, g, link, b_row):
    n0, rows = q_row.shape[1], b_row.shape[1]
    return pl.pallas_call(
        main_kernel,
        out_shape=(
            jax.ShapeDtypeStruct((1, n0), F32),
            jax.ShapeDtypeStruct((1, rows), F32),
        ),
        in_specs=[pl.BlockSpec(memory_space=pltpu.VMEM)] * 4
        + [pl.BlockSpec(memory_space=pl.ANY)]
        + [pl.BlockSpec(memory_space=pltpu.VMEM)] * 2,
        scratch_shapes=[pltpu.VMEM((n0, n0), F32), pltpu.VMEM((rows, rows), F32)]
        + [pltpu.VMEM((1, n0), F32)] * 4
        + [pltpu.VMEM((8, B), F32), pltpu.SemaphoreType.DMA],
        compiler_params=pltpu.CompilerParams(vmem_limit_bytes=WIDE_VMEM),
        name="main_solve",
    )(mine, other, q_row, c_row, g, link, b_row)


def primal_kernel(tallies_ref, w_ref, d_ref, dual_ref, back_ref, y_ref, out_ref):
    held = tallies_ref[lax.axis_index("scen")]
    scale = d_ref[...].astype(F32)
    for slot, source in enumerate((dual_ref, back_ref)):
        at = slice(slot, slot + 1)

        @pl.when(held > slot)
        def _(slot=slot, source=source, at=at):
            y_ref[at, :] = source[...]
            out_ref[at, :] = scale[at] * mm(source[...].astype(BF16), w_ref[slot])

        @pl.when(held <= slot)
        def _(at=at):
            y_ref[at, :] = jnp.zeros((1, y_ref.shape[1]), F32)
            out_ref[at, :] = jnp.zeros((1, out_ref.shape[1]), F32)


def primal(tallies, matrices, ratios, dual, back):
    return pl.pallas_call(
        primal_kernel,
        in_specs=[pl.BlockSpec(memory_space=pltpu.SMEM)]
        + [pl.BlockSpec(memory_space=pltpu.VMEM)] * 4,
        out_shape=(
            jax.ShapeDtypeStruct((2, dual.shape[1]), F32),
            jax.ShapeDtypeStruct(ratios.shape, F32),
        ),
        compiler_params=pltpu.CompilerParams(vmem_limit_bytes=VMEM),
        name="primal",
    )(tallies, matrices, ratios, dual, back)


def local(
    scen_size, col_size, matrices, ratios, damping, coupler, bounds, q_diag, c_vec, tallies
):
    n_s, n_z = scen_size, col_size
    rows = matrices.shape[1]
    n0 = coupler.shape[2]
    pos = lax.axis_index("scen")
    zpos = lax.axis_index("col")
    held = tallies[pos]
    own = held >= 1
    live = own | (tallies[pos ^ 1] == 2)
    partner = [(i, i ^ 1) for i in range(n_s)]

    def everyone(x, axis, count, **kw):
        return lax.all_to_all(
            jnp.broadcast_to(x[None], (count,) + x.shape), axis, 0, 0, **kw
        )

    gram1 = gram(1, n_z, matrices[1], ratios)
    later, gram1 = lax.optimization_barrier((matrices, gram1))
    gram_moved = lax.ppermute(gram1, "scen", partner)
    gram0 = gram(0, n_z, later[0], ratios)
    partial = choose(tallies, gram0, gram_moved).astype(F16)
    partial, coupler, damping, bounds = lax.optimization_barrier(
        (partial, coupler, damping, bounds)
    )
    sides = [
        jnp.concatenate([coupler[k], damping[k : k + 1], bounds[k : k + 1]], axis=0)
        for k in range(2)
    ]
    side_moved = lax.ppermute(sides[1], "scen", partner)
    side = jnp.where(own, sides[0], side_moved)
    link = side[:rows]
    reg_row = side[rows : rows + 1].astype(F32)
    b_row = side[rows + 1 : rows + 2].astype(F32)
    share = n0 // n_z
    width = -(-(share + 1) // B) * B
    rhs = jnp.concatenate(
        [
            lax.dynamic_slice(link, (0, zpos * share), (rows, share)),
            side[rows + 1][:, None],
            jnp.zeros((rows, width - share - 1), BF16),
        ],
        axis=1,
    )
    rhs = jnp.where(live, rhs, jnp.zeros_like(rhs))

    received = lax.all_to_all(partial, "col", 0, 0).astype(F32)
    whole = everyone(jnp.sum(received, axis=0).astype(F16), "col", n_z)
    g, terms = solve(whole.astype(F32), reg_row, rhs, link)

    count = n_s // 2
    same = [[2 * i + k for i in range(count)] for k in range(2)]
    terms = terms.reshape((n_s,) + terms.shape[2:])
    mine = lax.all_to_all(terms, "scen", 0, 0, axis_index_groups=[same[0] + same[1]])
    rows_of = [[k * n_z + z for k in group for z in range(n_z)] for group in same]
    half = everyone(
        jnp.sum(mine, axis=0).astype(F16), ("scen", "col"), count * n_z, axis_index_groups=rows_of
    )
    half = half.reshape((count, n_z) + half.shape[1:])
    other = lax.ppermute(half, "scen", partner)
    first, dual = main_solve(half.astype(F32), other.astype(F32), q_diag[None], c_vec[None], g, link, b_row)

    returned = lax.ppermute(dual, "scen", partner)
    duals, primals = primal(tallies, matrices, ratios, dual, returned)
    return first[0], duals, primals


def solution(mesh):
    body = functools.partial(local, mesh.shape["scen"], mesh.shape["col"])
    return jax.shard_map(
        body,
        mesh=mesh,
        in_specs=(
            P("scen", None, "col"),
            P("scen", "col"),
            P("scen", None),
            P("scen", None, None),
            P("scen", None),
            P(),
            P(),
            P(),
        ),
        out_specs=(P(), P("scen", None), P("scen", "col")),
        check_vma=False,
    )
```
